128 devices in a mesh: expert: 16 (over y, z_lo, core), shard: 8 (over z_hi, x).
Axes of the slice: x: 4, y: 4, z: 4 (z_hi: 2, z_lo: 2; z = z_hi * 2 + z_lo), core: 2. Of those that a mesh axis runs over, the one named last changes fastest.
Arguments:
- tokens: bfloat16 [16384, 2048], P(('expert', 'shard')), may hold values from -6 to 6
- expert_ids: int32 [16384, 4], P(('expert', 'shard')), may hold values from 0 to 15, all different within a row; in each aligned block of 128 rows (0 to 127, 128 to 255, ...) at most 48 rows name the same one
- route_weights: float32 [16384, 4], P(('expert', 'shard')), may hold values from 0.1 to 1
- partner: int32 [16], replicated, may hold values from 0 to 15, as said below
- w_in: bfloat16 [16, 2, 2048, 768], P('expert', None, 'shard'), may hold values from -0.125 to 0.125
- w_down: bfloat16 [16, 768, 2048], P('expert', None, 'shard'), may hold values from -0.21875 to 0.21875
- m_in: float32 [16, 2, 2048, 768], P('expert', None, 'shard'), may hold values from -6 to 6
- v_in: float32 [16, 2, 2048, 768], P('expert', None, 'shard'), may hold values from 0.01 to 1
- m_down: float32 [16, 768, 2048], P('expert', None, 'shard'), may hold values from -6 to 6
- v_down: float32 [16, 768, 2048], P('expert', None, 'shard'), may hold values from 0.01 to 1
- cotangent: bfloat16 [16384, 2048], P(('expert', 'shard')), may hold values from -6 to 6
Outputs:
- mixed: bfloat16 [16384, 2048], P(('expert', 'shard'))
- token_grad: bfloat16 [16384, 2048], P(('expert', 'shard'))
- new_w_in: bfloat16 [16, 2, 2048, 768], P('expert', None, 'shard')
- new_w_down: bfloat16 [16, 768, 2048], P('expert', None, 'shard')
- new_m_in: float32 [16, 2, 2048, 768], P('expert', None, 'shard')
- new_v_in: float32 [16, 2, 2048, 768], P('expert', None, 'shard')
- new_m_down: float32 [16, 768, 2048], P('expert', None, 'shard')
- new_v_down: float32 [16, 768, 2048], P('expert', None, 'shard')
The draws below stay inside these ranges and needn't reach their ends.
Inputs may be any that keep to these rules, and one draw needn't show every extreme that they name: `expert_ids`: within the rows of one device no expert is named more than 48 times, a bound that some block reaches. partner[g] is g or (g + 8) mod 16, and partner[partner[g]] = g; partner[0] is 8.
All inputs are finite; a program needn't handle non-finite values.
Results may differ from the reference program's by a relative error of at most 0.024.
Values may be sent and summed in bfloat16 or wider, within the bound.
A program may use at most 128 MiB of HBM per device.

```python
import math
import jax
import jax.numpy as jnp
import numpy as np
from jax import lax

D = 2048
FF = 768
TOP = 4
TOK_DEV = 128
EXPERTS = 16
CAP = 48
TOKENS = 16384
N_EXPERT = 16
N_SHARD = 8


def draw_partner(key, part):
    halfway = EXPERTS // 2
    flag_bits = jax.random.randint(key, (halfway,), 0, 2).astype(jnp.int32)
    flag_bits = flag_bits.at[0].set(1)
    doubled = jnp.concatenate([flag_bits, flag_bits])
    identity = jnp.arange(EXPERTS, dtype=jnp.int32)
    return jnp.where(doubled == 1, (identity + halfway) % EXPERTS, identity).astype(jnp.int32)


def steps_of(stream_key, dims, cuts, smallest, high):
    def one(axis_at, parts):
        steps = jax.random.uniform(jax.random.fold_in(jax.random.fold_in(stream_key, 6), axis_at), (parts,), jnp.float32, smallest / len(cuts), high / len(cuts))
        return jnp.repeat(jnp.exp(steps), dims[axis_at] // parts).reshape((-1,) + (1,) * (len(dims) - axis_at - 1))

    factor_of = one(*cuts[0])
    for cut in cuts[1:]:
        factor_of = factor_of * one(*cut)
    return factor_of


def assign_block(own_key, own, number, rows, amount, top, reach, lean):
    order = jax.random.permutation(own_key, amount)
    heavy_load, ordinary = shares(amount, rows * top, reach, lean, True), shares(amount, rows * top, reach, lean, False)
    places = jnp.arange(amount)

    def named(lengths, rotation):
        used = int((lengths > 0).sum())
        fixed = max(1, used // 4)
        shifted = fixed + (places - fixed + rotation * (used - fixed)) % max(1, amount - fixed)
        return jnp.zeros((amount,), jnp.int32).at[order[jnp.where(places < fixed, places, shifted)]].set(jnp.asarray(lengths, jnp.int32))

    lengths = jnp.where(number % 4 == 0, named(heavy_load, number // 4), named(ordinary, number - number // 4 - 1))
    mixed = jax.random.permutation(jax.random.fold_in(own, 3), amount)
    source_of, receiver = mixed[0:amount // 2 * 2:2], mixed[1:amount // 2 * 2:2]
    slack = jnp.minimum(lengths[source_of] - 1, reach - lengths[receiver]) // 2
    slack = jnp.where((source_of == order[0]) | (receiver == order[0]) | (lengths[receiver] == 0), 0, jnp.maximum(slack, 0))
    shifted = jax.random.randint(jax.random.fold_in(own, 4), (amount // 2,), 0, 1 << 20) % (slack + 1)
    lengths = lengths.at[source_of].add(-shifted).at[receiver].add(shifted)
    labels = jnp.searchsorted(jnp.cumsum(lengths), jnp.arange(rows * top), side="right").astype(jnp.int32)
    grid = labels.reshape(top, rows).T
    grid = grid[jax.random.permutation(jax.random.fold_in(own, 1), rows)]
    rotation = jax.random.randint(jax.random.fold_in(own, 2), (rows, 1), 0, top)
    return jnp.take_along_axis(grid, (jnp.arange(top)[None, :] + rotation) % top, axis=1)


def shares(number_of, total, most, lean, full):
    loads = [(1 << 20) // math.isqrt(rank ** lean) + 1 for rank in range(1, number_of + 1)]
    largest = most if full else min(most, max(-(-total // number_of), total * loads[0] // sum(loads)))
    least = 1 if total - largest >= number_of - 1 else 0
    given, rest = [largest] + [least] * (number_of - 1), total - largest - least * (number_of - 1)
    while rest > 0:
        free = [i for i in range(1, number_of) if given[i] < largest] or [i for i in range(1, number_of) if given[i] < most]
        whole, remaining = sum([loads[i] for i in free]), rest
        for i in free:
            extra = min(most - given[i], max(1, remaining * loads[i] // whole), rest)
            given[i] = given[i] + extra
            rest = rest - extra
    return np.array(given)


def scatter_about(rng, shape, width, reach, cuts=(), kind=jnp.bfloat16):
    values = width * jax.random.normal(rng, shape, jnp.float32)
    if cuts:
        values = values * steps_of(rng, shape, cuts, -0.22, 0.18)
    return jnp.clip(values, -reach, reach).astype(kind)


def setup_inputs(seed: int = 0) -> dict:
    key_of = jax.random.split(jax.random.key(seed), 12)
    tokens = scatter_about(key_of[0], (TOKENS, D), 1.0, 6.0, ((0, 128),))
    expert_ids_keys = jax.random.split(jax.random.fold_in(key_of[1], 1), TOKENS // TOK_DEV)
    expert_ids_turns = jax.random.permutation(jax.random.fold_in(key_of[1], 3), TOKENS // TOK_DEV)
    expert_ids = jax.vmap(lambda own, number: assign_block(jax.random.fold_in(key_of[1], 2), own, number, TOK_DEV, EXPERTS, TOP, CAP, 2))(expert_ids_keys, expert_ids_turns).reshape((TOKENS, TOP))
    route_weights = jnp.clip(0.1 + 0.9 * jax.random.uniform(key_of[2], (TOKENS, TOP), jnp.float32) ** steps_of(key_of[2], (TOKENS, TOP), ((0, 128),), -0.2, 0.2), 0.1, 1.0)
    partner = draw_partner(jax.random.fold_in(key_of[11], 71), 0)
    w_in = scatter_about(key_of[4], (EXPERTS, 2, D, FF), D ** -0.5, 0.125, ((0, 16), (2, 8)))
    w_down = scatter_about(key_of[5], (EXPERTS, FF, D), FF ** -0.5, 0.21875, ((0, 16), (2, 8)))
    m_in = scatter_about(key_of[6], (EXPERTS, 2, D, FF), 0.5, 6.0, ((0, 16), (2, 8)), jnp.float32)
    v_in = jnp.clip(jnp.exp(math.log(1.0) - 4.6051702 * jax.random.uniform(key_of[7], (EXPERTS, 2, D, FF), jnp.float32) ** steps_of(key_of[7], (EXPERTS, 2, D, FF), ((0, 16), (2, 8)), -0.2, 0.2)), 0.01, 1.0)
    m_down = scatter_about(key_of[8], (EXPERTS, FF, D), 0.5, 6.0, ((0, 16), (2, 8)), jnp.float32)
    v_down = jnp.clip(jnp.exp(math.log(1.0) - 4.6051702 * jax.random.uniform(key_of[9], (EXPERTS, FF, D), jnp.float32) ** steps_of(key_of[9], (EXPERTS, FF, D), ((0, 16), (2, 8)), -0.2, 0.2)), 0.01, 1.0)
    cotangent = scatter_about(key_of[10], (TOKENS, D), 1.0, 6.0, ((0, 128),))
    return dict(tokens=tokens, expert_ids=expert_ids, route_weights=route_weights, partner=partner, w_in=w_in, w_down=w_down, m_in=m_in, v_in=v_in, m_down=m_down, v_down=v_down, cotangent=cotangent)


beta_first = 0.9
beta_second = 0.999
learn_rate = 0.01
adam_eps = 1e-08
bias_first = 0.9999734386011124
bias_second = 0.09520785288629038

def silu_parts(gate_pre):
    sigmoid_value = jax.nn.sigmoid(gate_pre)
    silu_value = gate_pre * sigmoid_value
    slope = sigmoid_value * (1.0 + gate_pre * (1.0 - sigmoid_value))
    return (silu_value, slope)

def adam_update(weight, first, second, grad):
    first_new = beta_first * first + (1.0 - beta_first) * grad
    second_new = beta_second * second + (1.0 - beta_second) * grad * grad
    update = learn_rate * (first_new / bias_first) / (jnp.sqrt(second_new / bias_second) + adam_eps)
    return ((weight.astype(jnp.float32) - update).astype(jnp.bfloat16), first_new, second_new)

def rounded(values):
    return lax.optimization_barrier(values.astype(jnp.bfloat16)).astype(jnp.float32)

def by_group(array):
    last = array.shape[-1]
    split = array.reshape(N_EXPERT, N_SHARD, CAP, last)
    return jnp.swapaxes(split, 0, 1).reshape(N_SHARD, N_EXPERT * CAP, last)

def reference(tokens, expert_ids, route_weights, partner, w_in, w_down, m_in, v_in, m_down, v_down, cotangent):
    devices_all = N_EXPERT * N_SHARD
    entries = TOK_DEV * TOP
    per_device = expert_ids.reshape(devices_all, entries)
    expert_range = jnp.arange(EXPERTS, dtype=jnp.int32)
    onehot = (per_device[:, :, None] == expert_range[None, None, :]).astype(jnp.int32)
    before = jnp.cumsum(onehot, axis=1) - onehot
    slot_index = lax.optimization_barrier(jnp.sum(before * onehot, axis=2)).astype(jnp.int32)
    device_rows = jnp.broadcast_to(jnp.arange(devices_all, dtype=jnp.int32)[:, None], (devices_all, entries))
    entry_global = device_rows * entries + jnp.arange(entries, dtype=jnp.int32)[None, :]
    filler = jnp.full((devices_all, EXPERTS, CAP), -1, jnp.int32).at[device_rows, per_device, slot_index].set(entry_global)
    flat_weights = route_weights.reshape(-1)

    def expert_step(carry, expert):
        mixed_sum, grad_sum = carry
        fill = lax.dynamic_index_in_dim(filler, expert, 1, keepdims=False).reshape(-1)
        valid = fill >= 0
        safe = jnp.maximum(fill, 0).astype(jnp.int32)
        token_rows = (safe // TOP).astype(jnp.int32)
        weight_sel = jnp.where(valid, flat_weights[safe], jnp.zeros((), flat_weights.dtype))
        rows_x = jnp.where(valid[:, None], tokens[token_rows], jnp.zeros((), tokens.dtype))
        dout_rows = (weight_sel[:, None] * cotangent[token_rows].astype(jnp.float32)).astype(jnp.bfloat16)
        in_weight = lax.dynamic_index_in_dim(w_in, expert, 0, keepdims=False)
        down_weight = lax.dynamic_index_in_dim(w_down, expert, 0, keepdims=False)
        gate_pre = jnp.dot(rows_x, in_weight[0], preferred_element_type=jnp.float32)
        up_pre = jnp.dot(rows_x, in_weight[1], preferred_element_type=jnp.float32)
        silu_value, slope = silu_parts(gate_pre)
        hidden = (silu_value * up_pre).astype(jnp.bfloat16)
        expert_out = jnp.dot(hidden, down_weight, preferred_element_type=jnp.float32).astype(jnp.bfloat16)
        mixed_sum = mixed_sum.at[token_rows].add(weight_sel[:, None] * expert_out.astype(jnp.float32))
        grad_hidden = jnp.dot(dout_rows, down_weight.T, preferred_element_type=jnp.float32)
        grad_gate = (grad_hidden * up_pre * slope).astype(jnp.bfloat16)
        grad_up = (grad_hidden * silu_value).astype(jnp.bfloat16)
        entry_grad = (jnp.dot(grad_gate, in_weight[0].T, preferred_element_type=jnp.float32) + jnp.dot(grad_up, in_weight[1].T, preferred_element_type=jnp.float32)).astype(jnp.bfloat16)
        grad_sum = grad_sum.at[token_rows].add(entry_grad.astype(jnp.float32))
        grad_both = jnp.concatenate([grad_gate, grad_up], axis=1)
        pieces = (by_group(rows_x), by_group(grad_both), by_group(hidden), by_group(dout_rows))

        def group_step(totals, piece):
            x_part, both_part, hidden_part, dout_part = piece
            in_term = rounded(jnp.dot(x_part.T, both_part, preferred_element_type=jnp.float32))
            down_term = rounded(jnp.dot(hidden_part.T, dout_part, preferred_element_type=jnp.float32))
            return ((totals[0] + in_term, totals[1] + down_term), None)
        start_totals = (jnp.zeros((D, 2 * FF), jnp.float32), jnp.zeros((FF, D), jnp.float32))
        totals, unused = lax.scan(group_step, start_totals, pieces)
        grad_in = jnp.transpose(totals[0].reshape(D, 2, FF), (1, 0, 2))
        grad_down = totals[1]
        new_in, first_in, second_in = adam_update(in_weight, lax.dynamic_index_in_dim(m_in, expert, 0, keepdims=False), lax.dynamic_index_in_dim(v_in, expert, 0, keepdims=False), grad_in)
        new_down, first_down, second_down = adam_update(down_weight, lax.dynamic_index_in_dim(m_down, expert, 0, keepdims=False), lax.dynamic_index_in_dim(v_down, expert, 0, keepdims=False), grad_down)
        return ((mixed_sum, grad_sum), (new_in, new_down, first_in, second_in, first_down, second_down))
    start = (jnp.zeros((TOKENS, D), jnp.float32), jnp.zeros((TOKENS, D), jnp.float32))
    sums, states = lax.scan(expert_step, start, expert_range)
    placed = tuple((jnp.take(state, partner.astype(jnp.int32), axis=0) for state in states))
    return (sums[0].astype(jnp.bfloat16), sums[1].astype(jnp.bfloat16), placed[0], placed[1], placed[2], placed[3], placed[4], placed[5])
```

```python
import jax
import jax.numpy as jnp
from jax import lax
from jax.sharding import PartitionSpec as P

beta_first = 0.9
beta_second = 0.999
learn_rate = 0.01
adam_eps = 1e-08
bias_first = 0.9999734386011124
bias_second = 0.09520785288629038


def shifted(block, axis, distance):
    devices = range(lax.axis_size(axis))
    route = [((i - distance) % len(devices), i) for i in devices]
    return lax.ppermute(block, axis, route)


def silu_parts(gate_pre):
    sigmoid_value = jax.nn.sigmoid(gate_pre)
    silu_value = gate_pre * sigmoid_value
    slope = sigmoid_value * (1.0 + gate_pre * (1.0 - sigmoid_value))
    return (silu_value, slope)


def adam_update(weight, first, second, grad):
    first_new = beta_first * first + (1.0 - beta_first) * grad
    second_new = beta_second * second + (1.0 - beta_second) * grad * grad
    update = learn_rate * (first_new / bias_first) / (jnp.sqrt(second_new / bias_second) + adam_eps)
    return ((weight.astype(jnp.float32) - update).astype(jnp.bfloat16), first_new, second_new)


def route_table(expert_ids, dest_rows, groups, capacity):
    entry_count = expert_ids.shape[0] * expert_ids.shape[1]
    flat_ids = expert_ids.reshape(entry_count)
    onehot = (flat_ids[:, None] == jnp.arange(groups, dtype=jnp.int32)[None, :]).astype(jnp.int32)
    before = jnp.cumsum(onehot, axis=0) - onehot
    slot_index = jnp.sum(before * onehot, axis=1)
    position = dest_rows.reshape(entry_count) * capacity + slot_index
    entry_index = jnp.arange(entry_count, dtype=jnp.int32)
    filler = jnp.full((groups * capacity,), -1, jnp.int32).at[position].set(entry_index)
    return (position, filler)


def fill_rows(source_rows, filler, groups, capacity):
    picked = jnp.take(source_rows, jnp.maximum(filler, 0), axis=0)
    kept = jnp.where((filler >= 0)[:, None], picked, jnp.zeros_like(picked))
    return kept.reshape(groups, capacity, source_rows.shape[1])


def contract_rows(left, right):
    return lax.dot_general(
        left, right, (((0,), (0,)), ((), ())), preferred_element_type=jnp.float32
    )


def contract_cols(left, right):
    return lax.dot_general(
        left, right, (((1,), (1,)), ((), ())), preferred_element_type=jnp.float32
    )


def body(
    tokens, expert_ids, route_weights, partner, w_in, w_down, m_in, v_in, m_down, v_down, cotangent
):
    groups = lax.axis_size("expert")
    halfway = groups // 2
    tok_rows = tokens.shape[0]
    width = tokens.shape[1]
    top_count = expert_ids.shape[1]
    capacity = 3 * tok_rows * top_count // (2 * groups)
    row_index = lax.axis_index("expert")
    expert_range = jnp.arange(groups, dtype=jnp.int32)
    own_partner = jnp.sum(jnp.where(expert_range == row_index, partner, 0))
    take_other = own_partner != row_index
    moved_weights = shifted((w_in, w_down), "expert", halfway)
    w_in, w_down = (
        jnp.where(take_other, moved, owned) for moved, owned in zip(moved_weights, (w_in, w_down))
    )
    moved_states = tuple(
        shifted(state.astype(jnp.bfloat16), "expert", halfway).astype(state.dtype)
        for state in (m_in, v_in, m_down, v_down)
    )
    m_in, v_in, m_down, v_down = (
        jnp.where(take_other, moved, owned)
        for moved, owned in zip(moved_states, (m_in, v_in, m_down, v_down))
    )
    in_full, down_full = (
        lax.all_gather(w_in, "shard", axis=2, tiled=True),
        lax.all_gather(w_down, "shard", axis=2, tiled=True),
    )
    gate_weight = in_full[0, 0]
    up_weight = in_full[0, 1]
    down_weight = down_full[0]
    hidden_width = gate_weight.shape[1]
    position, filler = route_table(expert_ids, partner[expert_ids], groups, capacity)
    token_fill = jnp.where(filler >= 0, filler // top_count, -1)
    send_rows = fill_rows(tokens, token_fill, groups, capacity)
    arrived = lax.all_to_all(send_rows, "expert", split_axis=0, concat_axis=0, tiled=True)
    rows_x = arrived.reshape(groups * capacity, width)
    own_moments = (m_in, v_in, m_down, v_down)
    gate_pre = jnp.dot(rows_x, gate_weight, preferred_element_type=jnp.float32)
    up_pre = jnp.dot(rows_x, up_weight, preferred_element_type=jnp.float32)
    silu_value, slope = silu_parts(gate_pre)
    hidden = (silu_value * up_pre).astype(jnp.bfloat16)
    expert_out = jnp.dot(hidden, down_weight, preferred_element_type=jnp.float32).astype(
        jnp.bfloat16
    )
    returned = lax.all_to_all(
        expert_out.reshape(groups, capacity, width),
        "expert",
        split_axis=0,
        concat_axis=0,
        tiled=True,
    )
    per_entry = jnp.take(returned.reshape(groups * capacity, width), position, axis=0).reshape(
        tok_rows, top_count, width
    )
    mixed = jnp.sum(route_weights[:, :, None] * per_entry.astype(jnp.float32), axis=1).astype(
        jnp.bfloat16
    )
    scaled = (route_weights[:, :, None] * cotangent[:, None, :].astype(jnp.float32)).astype(
        jnp.bfloat16
    )
    send_grads = fill_rows(scaled.reshape(tok_rows * top_count, width), filler, groups, capacity)
    dout_rows = lax.all_to_all(
        send_grads, "expert", split_axis=0, concat_axis=0, tiled=True
    ).reshape(groups * capacity, width)
    grad_hidden = contract_cols(dout_rows, down_weight)
    grad_gate = (grad_hidden * up_pre * slope).astype(jnp.bfloat16)
    grad_up = (grad_hidden * silu_value).astype(jnp.bfloat16)
    entry_grads = (
        contract_cols(grad_gate, gate_weight) + contract_cols(grad_up, up_weight)
    ).astype(jnp.bfloat16)
    back_rows = lax.all_to_all(
        entry_grads.reshape(groups, capacity, width),
        "expert",
        split_axis=0,
        concat_axis=0,
        tiled=True,
    )
    per_back = jnp.take(back_rows.reshape(groups * capacity, width), position, axis=0).reshape(
        tok_rows, top_count, width
    )
    token_grad = jnp.sum(per_back.astype(jnp.float32), axis=1).astype(jnp.bfloat16)
    grad_both = jnp.concatenate([grad_gate, grad_up], axis=1)
    share_rows = width // lax.axis_size("shard")
    shares = lax.psum_scatter(
        jnp.concatenate(
            [contract_rows(rows_x, grad_both), contract_rows(dout_rows, hidden)], axis=1
        ).astype(jnp.bfloat16),
        "shard",
        scatter_dimension=0,
        tiled=True,
    ).astype(jnp.float32)
    grad_in = jnp.transpose(
        shares[:, : 2 * hidden_width].reshape(share_rows, 2, hidden_width), (1, 0, 2)
    )[None]
    grad_down = jnp.transpose(shares[:, 2 * hidden_width :])[None]
    new_in, first_in, second_in = adam_update(w_in, own_moments[0], own_moments[1], grad_in)
    new_down, first_down, second_down = adam_update(
        w_down, own_moments[2], own_moments[3], grad_down
    )
    return (mixed, token_grad, new_in, new_down, first_in, second_in, first_down, second_down)


def solution(mesh):
    placed = (
        P(("expert", "shard"), None),
        P(("expert", "shard"), None),
        P(("expert", "shard"), None),
        P(),
        P("expert", None, "shard", None),
        P("expert", None, "shard"),
        P("expert", None, "shard", None),
        P("expert", None, "shard", None),
        P("expert", None, "shard"),
        P("expert", None, "shard"),
        P(("expert", "shard"), None),
    )
    return jax.shard_map(
        body,
        mesh=mesh,
        in_specs=placed,
        out_specs=(
            P(("expert", "shard"), None),
            P(("expert", "shard"), None),
            P("expert", None, "shard", None),
            P("expert", None, "shard"),
            P("expert", None, "shard", None),
            P("expert", None, "shard", None),
            P("expert", None, "shard"),
            P("expert", None, "shard"),
        ),
        check_vma=False,
    )
```

```python
import jax
import jax.numpy as jnp
from jax import lax
from jax.sharding import PartitionSpec as P

beta_first = 0.9
beta_second = 0.999
learn_rate = 0.01
adam_eps = 1e-08
bias_first = 0.9999734386011124
bias_second = 0.09520785288629038


def shifted(block, axis, distance):
    devices = range(lax.axis_size(axis))
    route = [((i - distance) % len(devices), i) for i in devices]
    return lax.ppermute(block, axis, route)


def gather_shards(block, axis, dim):
    count = lax.axis_size(axis)
    me = lax.axis_index(axis)
    arrived = [block] + [
        lax.ppermute(block, axis, [(i, (i + k) % count) for i in range(count)])
        for k in range(1, count)
    ]
    order = (me - jnp.arange(count, dtype=jnp.int32)) % count
    stacked = jnp.take(jnp.stack(arrived), order, axis=0)
    return jnp.concatenate([stacked[j] for j in range(count)], axis=dim)


def scatter_sum(partial, axis):
    count = lax.axis_size(axis)
    me = lax.axis_index(axis)
    rows = partial.shape[0] // count
    chunks = partial.reshape(count, rows, partial.shape[1])
    total = jnp.take(chunks, me, axis=0).astype(jnp.float32)
    for k in range(1, count):
        piece = jnp.take(chunks, (me + k) % count, axis=0)
        total = total + lax.ppermute(
            piece, axis, [(i, (i + k) % count) for i in range(count)]
        ).astype(jnp.float32)
    return total


def silu_parts(gate_pre):
    sigmoid_value = jax.nn.sigmoid(gate_pre)
    silu_value = gate_pre * sigmoid_value
    slope = sigmoid_value * (1.0 + gate_pre * (1.0 - sigmoid_value))
    return (silu_value, slope)


def adam_update(weight, first, second, grad):
    first_new = beta_first * first + (1.0 - beta_first) * grad
    second_new = beta_second * second + (1.0 - beta_second) * grad * grad
    update = learn_rate * (first_new / bias_first) / (jnp.sqrt(second_new / bias_second) + adam_eps)
    return ((weight.astype(jnp.float32) - update).astype(jnp.bfloat16), first_new, second_new)


def route_table(expert_ids, dest_rows, groups, capacity):
    entry_count = expert_ids.shape[0] * expert_ids.shape[1]
    flat_ids = expert_ids.reshape(entry_count)
    onehot = (flat_ids[:, None] == jnp.arange(groups, dtype=jnp.int32)[None, :]).astype(jnp.int32)
    before = jnp.cumsum(onehot, axis=0) - onehot
    slot_index = jnp.sum(before * onehot, axis=1)
    position = dest_rows.reshape(entry_count) * capacity + slot_index
    entry_index = jnp.arange(entry_count, dtype=jnp.int32)
    filler = jnp.full((groups * capacity,), -1, jnp.int32).at[position].set(entry_index)
    return (position, filler)


def fill_rows(source_rows, filler, groups, capacity):
    picked = jnp.take(source_rows, jnp.maximum(filler, 0), axis=0)
    kept = jnp.where((filler >= 0)[:, None], picked, jnp.zeros_like(picked))
    return kept.reshape(groups, capacity, source_rows.shape[1])


def contract_rows(left, right):
    return lax.dot_general(
        left, right, (((0,), (0,)), ((), ())), preferred_element_type=jnp.float32
    )


def contract_cols(left, right):
    return lax.dot_general(
        left, right, (((1,), (1,)), ((), ())), preferred_element_type=jnp.float32
    )


def body(
    tokens, expert_ids, route_weights, partner, w_in, w_down, m_in, v_in, m_down, v_down, cotangent
):
    groups = lax.axis_size("expert")
    halfway = groups // 2
    tok_rows = tokens.shape[0]
    width = tokens.shape[1]
    top_count = expert_ids.shape[1]
    capacity = 3 * tok_rows * top_count // (2 * groups)
    row_index = lax.axis_index("expert")
    expert_range = jnp.arange(groups, dtype=jnp.int32)
    own_partner = jnp.sum(jnp.where(expert_range == row_index, partner, 0))
    take_other = own_partner != row_index
    moved_weights = shifted((w_in, w_down), "expert", halfway)
    w_in, w_down = (
        jnp.where(take_other, moved, owned) for moved, owned in zip(moved_weights, (w_in, w_down))
    )
    moved_states = tuple(
        shifted(state.astype(jnp.bfloat16), "expert", halfway).astype(state.dtype)
        for state in (m_in, v_in, m_down, v_down)
    )
    m_in, v_in, m_down, v_down = (
        jnp.where(take_other, moved, owned)
        for moved, owned in zip(moved_states, (m_in, v_in, m_down, v_down))
    )
    in_full, down_full = (gather_shards(w_in, "shard", 2), gather_shards(w_down, "shard", 2))
    gate_weight = in_full[0, 0]
    up_weight = in_full[0, 1]
    down_weight = down_full[0]
    hidden_width = gate_weight.shape[1]
    position, filler = route_table(expert_ids, partner[expert_ids], groups, capacity)
    token_fill = jnp.where(filler >= 0, filler // top_count, -1)
    send_rows = fill_rows(tokens, token_fill, groups, capacity)
    arrived = lax.all_to_all(send_rows, "expert", split_axis=0, concat_axis=0, tiled=True)
    rows_x = arrived.reshape(groups * capacity, width)
    own_moments = (m_in, v_in, m_down, v_down)
    gate_pre = jnp.dot(rows_x, gate_weight, preferred_element_type=jnp.float32)
    up_pre = jnp.dot(rows_x, up_weight, preferred_element_type=jnp.float32)
    silu_value, slope = silu_parts(gate_pre)
    hidden = (silu_value * up_pre).astype(jnp.bfloat16)
    expert_out = jnp.dot(hidden, down_weight, preferred_element_type=jnp.float32).astype(
        jnp.bfloat16
    )
    returned = lax.all_to_all(
        expert_out.reshape(groups, capacity, width),
        "expert",
        split_axis=0,
        concat_axis=0,
        tiled=True,
    )
    per_entry = jnp.take(returned.reshape(groups * capacity, width), position, axis=0).reshape(
        tok_rows, top_count, width
    )
    mixed = jnp.sum(route_weights[:, :, None] * per_entry.astype(jnp.float32), axis=1).astype(
        jnp.bfloat16
    )
    scaled = (route_weights[:, :, None] * cotangent[:, None, :].astype(jnp.float32)).astype(
        jnp.bfloat16
    )
    send_grads = fill_rows(scaled.reshape(tok_rows * top_count, width), filler, groups, capacity)
    dout_rows = lax.all_to_all(
        send_grads, "expert", split_axis=0, concat_axis=0, tiled=True
    ).reshape(groups * capacity, width)
    grad_hidden = contract_cols(dout_rows, down_weight)
    grad_gate = (grad_hidden * up_pre * slope).astype(jnp.bfloat16)
    grad_up = (grad_hidden * silu_value).astype(jnp.bfloat16)
    entry_grads = (
        contract_cols(grad_gate, gate_weight) + contract_cols(grad_up, up_weight)
    ).astype(jnp.bfloat16)
    back_rows = lax.all_to_all(
        entry_grads.reshape(groups, capacity, width),
        "expert",
        split_axis=0,
        concat_axis=0,
        tiled=True,
    )
    per_back = jnp.take(back_rows.reshape(groups * capacity, width), position, axis=0).reshape(
        tok_rows, top_count, width
    )
    token_grad = jnp.sum(per_back.astype(jnp.float32), axis=1).astype(jnp.bfloat16)
    grad_both = jnp.concatenate([grad_gate, grad_up], axis=1)
    share_rows = width // lax.axis_size("shard")
    shares = scatter_sum(
        jnp.concatenate(
            [contract_rows(rows_x, grad_both), contract_rows(dout_rows, hidden)], axis=1
        ).astype(jnp.bfloat16),
        "shard",
    )
    grad_in = jnp.transpose(
        shares[:, : 2 * hidden_width].reshape(share_rows, 2, hidden_width), (1, 0, 2)
    )[None]
    grad_down = jnp.transpose(shares[:, 2 * hidden_width :])[None]
    new_in, first_in, second_in = adam_update(w_in, own_moments[0], own_moments[1], grad_in)
    new_down, first_down, second_down = adam_update(
        w_down, own_moments[2], own_moments[3], grad_down
    )
    return (mixed, token_grad, new_in, new_down, first_in, second_in, first_down, second_down)


def solution(mesh):
    placed = (
        P(("expert", "shard"), None),
        P(("expert", "shard"), None),
        P(("expert", "shard"), None),
        P(),
        P("expert", None, "shard", None),
        P("expert", None, "shard"),
        P("expert", None, "shard", None),
        P("expert", None, "shard", None),
        P("expert", None, "shard"),
        P("expert", None, "shard"),
        P(("expert", "shard"), None),
    )
    return jax.shard_map(
        body,
        mesh=mesh,
        in_specs=placed,
        out_specs=(
            P(("expert", "shard"), None),
            P(("expert", "shard"), None),
            P("expert", None, "shard", None),
            P("expert", None, "shard"),
            P("expert", None, "shard", None),
            P("expert", None, "shard", None),
            P("expert", None, "shard"),
            P("expert", None, "shard"),
        ),
        check_vma=False,
    )
```

```python
import jax
import jax.numpy as jnp
from jax import lax
from jax.experimental import pallas as pl
from jax.experimental.pallas import tpu as pltpu
from jax.sharding import PartitionSpec as P
import functools

beta_first = 0.9
beta_second = 0.999
learn_rate = 0.01
adam_eps = 1e-08
bias_first = 0.9999734386011124
bias_second = 0.09520785288629038


def shifted(block, axis, distance):
    devices = range(lax.axis_size(axis))
    route = [((i - distance) % len(devices), i) for i in devices]
    return lax.ppermute(block, axis, route)


def exchange_kernel(count, spread, width, *refs):
    sources, targets = refs[:width], refs[width : 2 * width]
    send_sems, recv_sems, local_sems = refs[2 * width :]
    me = lax.axis_index("shard")
    row = lax.axis_index("expert")
    mesh_ids = pl.DeviceIdType.MESH
    barrier = pltpu.get_barrier_semaphore()
    for k in range(1, count):
        pl.semaphore_signal(
            barrier, inc=1, device_id=(row, lax.rem(me + k, count)), device_id_type=mesh_ids
        )
    pl.semaphore_wait(barrier, count - 1)
    copies = []
    for a in range(width):
        own = sources[a] if spread else sources[a].at[me]
        local = pltpu.make_async_copy(own, targets[a].at[me], local_sems.at[a])
        local.start()
        copies.append(local)
        for k in range(1, count):
            peer = lax.rem(me + k, count)
            remote = pltpu.make_async_remote_copy(
                src_ref=sources[a] if spread else sources[a].at[peer],
                dst_ref=targets[a].at[me],
                send_sem=send_sems.at[a, k - 1],
                recv_sem=recv_sems.at[a, k - 1],
                device_id=(row, peer),
                device_id_type=mesh_ids,
            )
            remote.start()
            copies.append(remote)
    for copy in copies:
        copy.wait()


def exchange(blocks, spread, ident):
    count = lax.axis_size("shard")
    width = len(blocks)
    shapes = tuple(
        jax.ShapeDtypeStruct((count,) + b.shape if spread else b.shape, b.dtype) for b in blocks
    )
    moved = sum(b.size * b.dtype.itemsize for b in blocks)
    return pl.pallas_call(
        functools.partial(exchange_kernel, count, spread, width),
        out_shape=shapes,
        in_specs=[pl.BlockSpec(memory_space=pl.ANY)] * width,
        out_specs=tuple(pl.BlockSpec(memory_space=pl.ANY) for _ in blocks),
        scratch_shapes=[
            pltpu.SemaphoreType.DMA((width, count - 1)),
            pltpu.SemaphoreType.DMA((width, count - 1)),
            pltpu.SemaphoreType.DMA((width,)),
        ],
        compiler_params=pltpu.CompilerParams(collective_id=ident, has_side_effects=True),
        cost_estimate=pl.CostEstimate(
            flops=0, transcendentals=0, bytes_accessed=2 * moved * (count if spread else 1)
        ),
    )(*blocks)


def silu_parts(gate_pre):
    sigmoid_value = jax.nn.sigmoid(gate_pre)
    silu_value = gate_pre * sigmoid_value
    slope = sigmoid_value * (1.0 + gate_pre * (1.0 - sigmoid_value))
    return (silu_value, slope)


def adam_update(weight, first, second, grad):
    first_new = beta_first * first + (1.0 - beta_first) * grad
    second_new = beta_second * second + (1.0 - beta_second) * grad * grad
    update = learn_rate * (first_new / bias_first) / (jnp.sqrt(second_new / bias_second) + adam_eps)
    return ((weight.astype(jnp.float32) - update).astype(jnp.bfloat16), first_new, second_new)


def route_table(expert_ids, dest_rows, groups, capacity):
    entry_count = expert_ids.shape[0] * expert_ids.shape[1]
    flat_ids = expert_ids.reshape(entry_count)
    onehot = (flat_ids[:, None] == jnp.arange(groups, dtype=jnp.int32)[None, :]).astype(jnp.int32)
    before = jnp.cumsum(onehot, axis=0) - onehot
    slot_index = jnp.sum(before * onehot, axis=1)
    position = dest_rows.reshape(entry_count) * capacity + slot_index
    entry_index = jnp.arange(entry_count, dtype=jnp.int32)
    filler = jnp.full((groups * capacity,), -1, jnp.int32).at[position].set(entry_index)
    return (position, filler)


def fill_rows(source_rows, filler, groups, capacity):
    picked = jnp.take(source_rows, jnp.maximum(filler, 0), axis=0)
    kept = jnp.where((filler >= 0)[:, None], picked, jnp.zeros_like(picked))
    return kept.reshape(groups, capacity, source_rows.shape[1])


def contract_rows(left, right):
    return lax.dot_general(
        left, right, (((0,), (0,)), ((), ())), preferred_element_type=jnp.float32
    )


def contract_cols(left, right):
    return lax.dot_general(
        left, right, (((1,), (1,)), ((), ())), preferred_element_type=jnp.float32
    )


def body(
    tokens, expert_ids, route_weights, partner, w_in, w_down, m_in, v_in, m_down, v_down, cotangent
):
    groups = lax.axis_size("expert")
    halfway = groups // 2
    tok_rows = tokens.shape[0]
    width = tokens.shape[1]
    top_count = expert_ids.shape[1]
    capacity = 3 * tok_rows * top_count // (2 * groups)
    row_index = lax.axis_index("expert")
    expert_range = jnp.arange(groups, dtype=jnp.int32)
    own_partner = jnp.sum(jnp.where(expert_range == row_index, partner, 0))
    take_other = own_partner != row_index
    moved_weights = shifted((w_in, w_down), "expert", halfway)
    w_in, w_down = (
        jnp.where(take_other, moved, owned) for moved, owned in zip(moved_weights, (w_in, w_down))
    )
    moved_states = tuple(
        shifted(state.astype(jnp.bfloat16), "expert", halfway).astype(state.dtype)
        for state in (m_in, v_in, m_down, v_down)
    )
    m_in, v_in, m_down, v_down = (
        jnp.where(take_other, moved, owned)
        for moved, owned in zip(moved_states, (m_in, v_in, m_down, v_down))
    )
    gate_parts, up_parts, down_parts = exchange((w_in[0, 0], w_in[0, 1], w_down[0]), True, 0)
    gate_weight = gate_parts.reshape(-1, gate_parts.shape[-1])
    up_weight = up_parts.reshape(-1, up_parts.shape[-1])
    down_weight = jnp.transpose(down_parts, (1, 0, 2)).reshape(down_parts.shape[1], -1)
    hidden_width = gate_weight.shape[1]
    position, filler = route_table(expert_ids, partner[expert_ids], groups, capacity)
    token_fill = jnp.where(filler >= 0, filler // top_count, -1)
    send_rows = fill_rows(tokens, token_fill, groups, capacity)
    arrived = lax.all_to_all(send_rows, "expert", split_axis=0, concat_axis=0, tiled=True)
    rows_x = arrived.reshape(groups * capacity, width)
    own_moments = (m_in, v_in, m_down, v_down)
    gate_pre = jnp.dot(rows_x, gate_weight, preferred_element_type=jnp.float32)
    up_pre = jnp.dot(rows_x, up_weight, preferred_element_type=jnp.float32)
    silu_value, slope = silu_parts(gate_pre)
    hidden = (silu_value * up_pre).astype(jnp.bfloat16)
    expert_out = jnp.dot(hidden, down_weight, preferred_element_type=jnp.float32).astype(
        jnp.bfloat16
    )
    returned = lax.all_to_all(
        expert_out.reshape(groups, capacity, width),
        "expert",
        split_axis=0,
        concat_axis=0,
        tiled=True,
    )
    per_entry = jnp.take(returned.reshape(groups * capacity, width), position, axis=0).reshape(
        tok_rows, top_count, width
    )
    mixed = jnp.sum(route_weights[:, :, None] * per_entry.astype(jnp.float32), axis=1).astype(
        jnp.bfloat16
    )
    scaled = (route_weights[:, :, None] * cotangent[:, None, :].astype(jnp.float32)).astype(
        jnp.bfloat16
    )
    send_grads = fill_rows(scaled.reshape(tok_rows * top_count, width), filler, groups, capacity)
    dout_rows = lax.all_to_all(
        send_grads, "expert", split_axis=0, concat_axis=0, tiled=True
    ).reshape(groups * capacity, width)
    grad_hidden = contract_cols(dout_rows, down_weight)
    grad_gate = (grad_hidden * up_pre * slope).astype(jnp.bfloat16)
    grad_up = (grad_hidden * silu_value).astype(jnp.bfloat16)
    entry_grads = (
        contract_cols(grad_gate, gate_weight) + contract_cols(grad_up, up_weight)
    ).astype(jnp.bfloat16)
    back_rows = lax.all_to_all(
        entry_grads.reshape(groups, capacity, width),
        "expert",
        split_axis=0,
        concat_axis=0,
        tiled=True,
    )
    per_back = jnp.take(back_rows.reshape(groups * capacity, width), position, axis=0).reshape(
        tok_rows, top_count, width
    )
    token_grad = jnp.sum(per_back.astype(jnp.float32), axis=1).astype(jnp.bfloat16)
    grad_both = jnp.concatenate([grad_gate, grad_up], axis=1)
    share_rows = width // lax.axis_size("shard")
    partial = jnp.concatenate(
        [contract_rows(rows_x, grad_both), contract_rows(dout_rows, hidden)], axis=1
    ).astype(jnp.bfloat16)
    shard_count = lax.axis_size("shard")
    (arrived_parts,) = exchange(
        (partial.reshape(shard_count, share_rows, partial.shape[1]),), False, 1
    )
    shares = jnp.sum(arrived_parts.astype(jnp.float32), axis=0)
    grad_in = jnp.transpose(
        shares[:, : 2 * hidden_width].reshape(share_rows, 2, hidden_width), (1, 0, 2)
    )[None]
    grad_down = jnp.transpose(shares[:, 2 * hidden_width :])[None]
    new_in, first_in, second_in = adam_update(w_in, own_moments[0], own_moments[1], grad_in)
    new_down, first_down, second_down = adam_update(
        w_down, own_moments[2], own_moments[3], grad_down
    )
    return (mixed, token_grad, new_in, new_down, first_in, second_in, first_down, second_down)


def solution(mesh):
    placed = (
        P(("expert", "shard"), None),
        P(("expert", "shard"), None),
        P(("expert", "shard"), None),
        P(),
        P("expert", None, "shard", None),
        P("expert", None, "shard"),
        P("expert", None, "shard", None),
        P("expert", None, "shard", None),
        P("expert", None, "shard"),
        P("expert", None, "shard"),
        P(("expert", "shard"), None),
    )
    return jax.shard_map(
        body,
        mesh=mesh,
        in_specs=placed,
        out_specs=(
            P(("expert", "shard"), None),
            P(("expert", "shard"), None),
            P("expert", None, "shard", None),
            P("expert", None, "shard"),
            P("expert", None, "shard", None),
            P("expert", None, "shard", None),
            P("expert", None, "shard"),
            P("expert", None, "shard"),
        ),
        check_vma=False,
    )
```

```python
import jax
import jax.numpy as jnp
from jax import lax
from jax.experimental import pallas as pl
from jax.experimental.pallas import tpu as pltpu
from jax.sharding import PartitionSpec as P
import functools

beta_first = 0.9
beta_second = 0.999
learn_rate = 0.01
adam_eps = 1e-08
bias_first = 0.9999734386011124
bias_second = 0.09520785288629038


def shifted(block, axis, distance):
    devices = range(lax.axis_size(axis))
    route = [((i - distance) % len(devices), i) for i in devices]
    return lax.ppermute(block, axis, route)


def exchange_kernel(count, spread, width, *refs):
    sources, targets = refs[:width], refs[width : 2 * width]
    send_sems, recv_sems, local_sems = refs[2 * width :]
    me = lax.axis_index("shard")
    row = lax.axis_index("expert")
    mesh_ids = pl.DeviceIdType.MESH
    barrier = pltpu.get_barrier_semaphore()
    for k in range(1, count):
        pl.semaphore_signal(
            barrier, inc=1, device_id=(row, lax.rem(me + k, count)), device_id_type=mesh_ids
        )
    pl.semaphore_wait(barrier, count - 1)
    copies = []
    for a in range(width):
        own = sources[a] if spread else sources[a].at[me]
        local = pltpu.make_async_copy(own, targets[a].at[me], local_sems.at[a])
        local.start()
        copies.append(local)
        for k in range(1, count):
            peer = lax.rem(me + k, count)
            remote = pltpu.make_async_remote_copy(
                src_ref=sources[a] if spread else sources[a].at[peer],
                dst_ref=targets[a].at[me],
                send_sem=send_sems.at[a, k - 1],
                recv_sem=recv_sems.at[a, k - 1],
                device_id=(row, peer),
                device_id_type=mesh_ids,
            )
            remote.start()
            copies.append(remote)
    for copy in copies:
        copy.wait()


def exchange(blocks, spread, ident):
    count = lax.axis_size("shard")
    width = len(blocks)
    shapes = tuple(
        jax.ShapeDtypeStruct((count,) + b.shape if spread else b.shape, b.dtype) for b in blocks
    )
    moved = sum(b.size * b.dtype.itemsize for b in blocks)
    return pl.pallas_call(
        functools.partial(exchange_kernel, count, spread, width),
        out_shape=shapes,
        in_specs=[pl.BlockSpec(memory_space=pl.ANY)] * width,
        out_specs=tuple(pl.BlockSpec(memory_space=pl.ANY) for _ in blocks),
        scratch_shapes=[
            pltpu.SemaphoreType.DMA((width, count - 1)),
            pltpu.SemaphoreType.DMA((width, count - 1)),
            pltpu.SemaphoreType.DMA((width,)),
        ],
        compiler_params=pltpu.CompilerParams(collective_id=ident, has_side_effects=True),
        cost_estimate=pl.CostEstimate(
            flops=0, transcendentals=0, bytes_accessed=2 * moved * (count if spread else 1)
        ),
    )(*blocks)


def silu_parts(gate_pre):
    sigmoid_value = jax.nn.sigmoid(gate_pre)
    silu_value = gate_pre * sigmoid_value
    slope = sigmoid_value * (1.0 + gate_pre * (1.0 - sigmoid_value))
    return (silu_value, slope)


def adam_update(weight, first, second, grad):
    first_new = beta_first * first + (1.0 - beta_first) * grad
    second_new = beta_second * second + (1.0 - beta_second) * grad * grad
    update = learn_rate * (first_new / bias_first) / (jnp.sqrt(second_new / bias_second) + adam_eps)
    return ((weight.astype(jnp.float32) - update).astype(jnp.bfloat16), first_new, second_new)


def route_table(expert_ids, dest_rows, groups, capacity):
    entry_count = expert_ids.shape[0] * expert_ids.shape[1]
    flat_ids = expert_ids.reshape(entry_count)
    onehot = (flat_ids[:, None] == jnp.arange(groups, dtype=jnp.int32)[None, :]).astype(jnp.int32)
    before = jnp.cumsum(onehot, axis=0) - onehot
    slot_index = jnp.sum(before * onehot, axis=1)
    position = dest_rows.reshape(entry_count) * capacity + slot_index
    entry_index = jnp.arange(entry_count, dtype=jnp.int32)
    filler = jnp.full((groups * capacity,), -1, jnp.int32).at[position].set(entry_index)
    return (position, filler)


def fill_rows(source_rows, filler, groups, capacity):
    picked = jnp.take(source_rows, jnp.maximum(filler, 0), axis=0)
    kept = jnp.where((filler >= 0)[:, None], picked, jnp.zeros_like(picked))
    return kept.reshape(groups, capacity, source_rows.shape[1])


def contract_rows(left, right):
    return lax.dot_general(
        left, right, (((0,), (0,)), ((), ())), preferred_element_type=jnp.float32
    )


def contract_cols(left, right):
    return lax.dot_general(
        left, right, (((1,), (1,)), ((), ())), preferred_element_type=jnp.float32
    )


def body(
    tokens, expert_ids, route_weights, partner, w_in, w_down, m_in, v_in, m_down, v_down, cotangent
):
    groups = lax.axis_size("expert")
    halfway = groups // 2
    tok_rows = tokens.shape[0]
    width = tokens.shape[1]
    top_count = expert_ids.shape[1]
    capacity = 3 * tok_rows * top_count // (2 * groups)
    row_index = lax.axis_index("expert")
    expert_range = jnp.arange(groups, dtype=jnp.int32)
    own_partner = jnp.sum(jnp.where(expert_range == row_index, partner, 0))
    take_other = own_partner != row_index
    moved_weights = shifted((w_in, w_down), "expert", halfway)
    kept_in, kept_down = (
        jnp.where(take_other, moved, owned) for moved, owned in zip(moved_weights, (w_in, w_down))
    )
    moved_states = tuple(
        shifted(state.astype(jnp.bfloat16), "expert", halfway).astype(state.dtype)
        for state in (m_in, v_in, m_down, v_down)
    )
    m_in, v_in, m_down, v_down = (
        jnp.where(take_other, moved, owned)
        for moved, owned in zip(moved_states, (m_in, v_in, m_down, v_down))
    )
    in_full, down_full = (
        lax.all_gather(w_in, "shard", axis=2, tiled=True),
        lax.all_gather(w_down, "shard", axis=2, tiled=True),
    )
    gate_weight = in_full[0, 0]
    up_weight = in_full[0, 1]
    down_weight = down_full[0]
    hidden_width = gate_weight.shape[1]
    position, filler = route_table(expert_ids, expert_ids, groups, capacity)
    token_fill = jnp.where(filler >= 0, filler // top_count, -1)
    send_rows = fill_rows(tokens, token_fill, groups, capacity)
    arrived = lax.all_to_all(send_rows, "expert", split_axis=0, concat_axis=0, tiled=True)
    rows_x = arrived.reshape(groups * capacity, width)
    own_moments = (m_in, v_in, m_down, v_down)
    gate_pre = jnp.dot(rows_x, gate_weight, preferred_element_type=jnp.float32)
    up_pre = jnp.dot(rows_x, up_weight, preferred_element_type=jnp.float32)
    silu_value, slope = silu_parts(gate_pre)
    hidden = (silu_value * up_pre).astype(jnp.bfloat16)
    expert_out = jnp.dot(hidden, down_weight, preferred_element_type=jnp.float32).astype(
        jnp.bfloat16
    )
    returned = lax.all_to_all(
        expert_out.reshape(groups, capacity, width),
        "expert",
        split_axis=0,
        concat_axis=0,
        tiled=True,
    )
    per_entry = jnp.take(returned.reshape(groups * capacity, width), position, axis=0).reshape(
        tok_rows, top_count, width
    )
    mixed = jnp.sum(route_weights[:, :, None] * per_entry.astype(jnp.float32), axis=1).astype(
        jnp.bfloat16
    )
    scaled = (route_weights[:, :, None] * cotangent[:, None, :].astype(jnp.float32)).astype(
        jnp.bfloat16
    )
    send_grads = fill_rows(scaled.reshape(tok_rows * top_count, width), filler, groups, capacity)
    dout_rows = lax.all_to_all(
        send_grads, "expert", split_axis=0, concat_axis=0, tiled=True
    ).reshape(groups * capacity, width)
    grad_hidden = contract_cols(dout_rows, down_weight)
    grad_gate = (grad_hidden * up_pre * slope).astype(jnp.bfloat16)
    grad_up = (grad_hidden * silu_value).astype(jnp.bfloat16)
    entry_grads = (
        contract_cols(grad_gate, gate_weight) + contract_cols(grad_up, up_weight)
    ).astype(jnp.bfloat16)
    back_rows = lax.all_to_all(
        entry_grads.reshape(groups, capacity, width),
        "expert",
        split_axis=0,
        concat_axis=0,
        tiled=True,
    )
    per_back = jnp.take(back_rows.reshape(groups * capacity, width), position, axis=0).reshape(
        tok_rows, top_count, width
    )
    token_grad = jnp.sum(per_back.astype(jnp.float32), axis=1).astype(jnp.bfloat16)
    grad_both = jnp.concatenate([grad_gate, grad_up], axis=1)
    share_rows = width // lax.axis_size("shard")
    partial = jnp.concatenate(
        [contract_rows(rows_x, grad_both), contract_rows(dout_rows, hidden)], axis=1
    ).astype(jnp.bfloat16)
    shard_count = lax.axis_size("shard")
    (arrived_parts,) = exchange(
        (partial.reshape(shard_count, share_rows, partial.shape[1]),), False, 1
    )
    summed = jnp.sum(arrived_parts.astype(jnp.float32), axis=0).astype(jnp.bfloat16)
    shares = jnp.where(take_other, shifted(summed, "expert", halfway), summed).astype(jnp.float32)
    grad_in = jnp.transpose(
        shares[:, : 2 * hidden_width].reshape(share_rows, 2, hidden_width), (1, 0, 2)
    )[None]
    grad_down = jnp.transpose(shares[:, 2 * hidden_width :])[None]
    new_in, first_in, second_in = adam_update(kept_in, own_moments[0], own_moments[1], grad_in)
    new_down, first_down, second_down = adam_update(
        kept_down, own_moments[2], own_moments[3], grad_down
    )
    return (mixed, token_grad, new_in, new_down, first_in, second_in, first_down, second_down)


def solution(mesh):
    placed = (
        P(("expert", "shard"), None),
        P(("expert", "shard"), None),
        P(("expert", "shard"), None),
        P(),
        P("expert", None, "shard", None),
        P("expert", None, "shard"),
        P("expert", None, "shard", None),
        P("expert", None, "shard", None),
        P("expert", None, "shard"),
        P("expert", None, "shard"),
        P(("expert", "shard"), None),
    )
    return jax.shard_map(
        body,
        mesh=mesh,
        in_specs=placed,
        out_specs=(
            P(("expert", "shard"), None),
            P(("expert", "shard"), None),
            P("expert", None, "shard", None),
            P("expert", None, "shard"),
            P("expert", None, "shard", None),
            P("expert", None, "shard", None),
            P("expert", None, "shard"),
            P("expert", None, "shard"),
        ),
        check_vma=False,
    )
```

```python
import jax
import jax.numpy as jnp
from jax import lax
from jax.experimental import pallas as pl
from jax.experimental.pallas import tpu as pltpu
from jax.sharding import PartitionSpec as P
import functools

beta_first = 0.9
beta_second = 0.999
learn_rate = 0.01
adam_eps = 1e-08
bias_first = 0.9999734386011124
bias_second = 0.09520785288629038


def shifted(block, axis, distance):
    devices = range(lax.axis_size(axis))
    route = [((i - distance) % len(devices), i) for i in devices]
    return lax.ppermute(block, axis, route)


def exchange_kernel(count, spread, width, *refs):
    sources, targets = refs[:width], refs[width : 2 * width]
    send_sems, recv_sems, local_sems = refs[2 * width :]
    me = lax.axis_index("shard")
    row = lax.axis_index("expert")
    mesh_ids = pl.DeviceIdType.MESH
    barrier = pltpu.get_barrier_semaphore()
    for k in range(1, count):
        pl.semaphore_signal(
            barrier, inc=1, device_id=(row, lax.rem(me + k, count)), device_id_type=mesh_ids
        )
    pl.semaphore_wait(barrier, count - 1)
    copies = []
    for a in range(width):
        own = sources[a] if spread else sources[a].at[me]
        local = pltpu.make_async_copy(own, targets[a].at[me], local_sems.at[a])
        local.start()
        copies.append(local)
        for k in range(1, count):
            peer = lax.rem(me + k, count)
            remote = pltpu.make_async_remote_copy(
                src_ref=sources[a] if spread else sources[a].at[peer],
                dst_ref=targets[a].at[me],
                send_sem=send_sems.at[a, k - 1],
                recv_sem=recv_sems.at[a, k - 1],
                device_id=(row, peer),
                device_id_type=mesh_ids,
            )
            remote.start()
            copies.append(remote)
    for copy in copies:
        copy.wait()


def exchange(blocks, spread, ident):
    count = lax.axis_size("shard")
    width = len(blocks)
    shapes = tuple(
        jax.ShapeDtypeStruct((count,) + b.shape if spread else b.shape, b.dtype) for b in blocks
    )
    moved = sum(b.size * b.dtype.itemsize for b in blocks)
    return pl.pallas_call(
        functools.partial(exchange_kernel, count, spread, width),
        out_shape=shapes,
        in_specs=[pl.BlockSpec(memory_space=pl.ANY)] * width,
        out_specs=tuple(pl.BlockSpec(memory_space=pl.ANY) for _ in blocks),
        scratch_shapes=[
            pltpu.SemaphoreType.DMA((width, count - 1)),
            pltpu.SemaphoreType.DMA((width, count - 1)),
            pltpu.SemaphoreType.DMA((width,)),
        ],
        compiler_params=pltpu.CompilerParams(collective_id=ident, has_side_effects=True),
        cost_estimate=pl.CostEstimate(
            flops=0, transcendentals=0, bytes_accessed=2 * moved * (count if spread else 1)
        ),
    )(*blocks)


def silu_parts(gate_pre):
    sigmoid_value = jax.nn.sigmoid(gate_pre)
    silu_value = gate_pre * sigmoid_value
    slope = sigmoid_value * (1.0 + gate_pre * (1.0 - sigmoid_value))
    return (silu_value, slope)


def adam_update(weight, first, second, grad):
    first_new = beta_first * first + (1.0 - beta_first) * grad
    second_new = beta_second * second + (1.0 - beta_second) * grad * grad
    update = learn_rate * (first_new / bias_first) / (jnp.sqrt(second_new / bias_second) + adam_eps)
    return ((weight.astype(jnp.float32) - update).astype(jnp.bfloat16), first_new, second_new)


def route_table(expert_ids, dest_rows, groups, capacity):
    entry_count = expert_ids.shape[0] * expert_ids.shape[1]
    flat_ids = expert_ids.reshape(entry_count)
    onehot = (flat_ids[:, None] == jnp.arange(groups, dtype=jnp.int32)[None, :]).astype(jnp.int32)
    before = jnp.cumsum(onehot, axis=0) - onehot
    slot_index = jnp.sum(before * onehot, axis=1)
    position = dest_rows.reshape(entry_count) * capacity + slot_index
    entry_index = jnp.arange(entry_count, dtype=jnp.int32)
    filler = jnp.full((groups * capacity,), -1, jnp.int32).at[position].set(entry_index)
    return (position, filler)


def fill_rows(source_rows, filler, groups, capacity):
    picked = jnp.take(source_rows, jnp.maximum(filler, 0), axis=0)
    kept = jnp.where((filler >= 0)[:, None], picked, jnp.zeros_like(picked))
    return kept.reshape(groups, capacity, source_rows.shape[1])


def contract_rows(left, right):
    return lax.dot_general(
        left, right, (((0,), (0,)), ((), ())), preferred_element_type=jnp.float32
    )


def contract_cols(left, right):
    return lax.dot_general(
        left, right, (((1,), (1,)), ((), ())), preferred_element_type=jnp.float32
    )


def body(
    tokens, expert_ids, route_weights, partner, w_in, w_down, m_in, v_in, m_down, v_down, cotangent
):
    groups = lax.axis_size("expert")
    halfway = groups // 2
    tok_rows = tokens.shape[0]
    width = tokens.shape[1]
    top_count = expert_ids.shape[1]
    capacity = 3 * tok_rows * top_count // (2 * groups)
    row_index = lax.axis_index("expert")
    expert_range = jnp.arange(groups, dtype=jnp.int32)
    own_partner = jnp.sum(jnp.where(expert_range == row_index, partner, 0))
    take_other = own_partner != row_index
    moved_weights = shifted((w_in, w_down), "expert", halfway)
    kept_in, kept_down = (
        jnp.where(take_other, moved, owned) for moved, owned in zip(moved_weights, (w_in, w_down))
    )
    moved_states = tuple(
        shifted(state.astype(jnp.bfloat16), "expert", halfway).astype(state.dtype)
        for state in (m_in, v_in, m_down, v_down)
    )
    m_in, v_in, m_down, v_down = (
        jnp.where(take_other, moved, owned)
        for moved, owned in zip(moved_states, (m_in, v_in, m_down, v_down))
    )
    gate_parts, up_parts, down_parts = exchange((w_in[0, 0], w_in[0, 1], w_down[0]), True, 0)
    (gate_parts, up_parts, down_parts), kept_in, kept_down, m_in, v_in, m_down, v_down = (
        lax.optimization_barrier(
            ((gate_parts, up_parts, down_parts), kept_in, kept_down, m_in, v_in, m_down, v_down)
        )
    )
    gate_weight = gate_parts.reshape(-1, gate_parts.shape[-1])
    up_weight = up_parts.reshape(-1, up_parts.shape[-1])
    down_weight = jnp.transpose(down_parts, (1, 0, 2)).reshape(down_parts.shape[1], -1)
    hidden_width = gate_weight.shape[1]
    position, filler = route_table(expert_ids, expert_ids, groups, capacity)
    token_fill = jnp.where(filler >= 0, filler // top_count, -1)
    send_rows = fill_rows(tokens, token_fill, groups, capacity)
    arrived = lax.all_to_all(send_rows, "expert", split_axis=0, concat_axis=0, tiled=True)
    rows_x = arrived.reshape(groups * capacity, width)
    own_moments = (m_in, v_in, m_down, v_down)
    gate_pre = jnp.dot(rows_x, gate_weight, preferred_element_type=jnp.float32)
    up_pre = jnp.dot(rows_x, up_weight, preferred_element_type=jnp.float32)
    silu_value, slope = silu_parts(gate_pre)
    hidden = (silu_value * up_pre).astype(jnp.bfloat16)
    expert_out = jnp.dot(hidden, down_weight, preferred_element_type=jnp.float32).astype(
        jnp.bfloat16
    )
    returned = lax.all_to_all(
        expert_out.reshape(groups, capacity, width),
        "expert",
        split_axis=0,
        concat_axis=0,
        tiled=True,
    )
    per_entry = jnp.take(returned.reshape(groups * capacity, width), position, axis=0).reshape(
        tok_rows, top_count, width
    )
    mixed = jnp.sum(route_weights[:, :, None] * per_entry.astype(jnp.float32), axis=1).astype(
        jnp.bfloat16
    )
    scaled = (route_weights[:, :, None] * cotangent[:, None, :].astype(jnp.float32)).astype(
        jnp.bfloat16
    )
    send_grads = fill_rows(scaled.reshape(tok_rows * top_count, width), filler, groups, capacity)
    dout_rows = lax.all_to_all(
        send_grads, "expert", split_axis=0, concat_axis=0, tiled=True
    ).reshape(groups * capacity, width)
    grad_hidden = contract_cols(dout_rows, down_weight)
    grad_gate = (grad_hidden * up_pre * slope).astype(jnp.bfloat16)
    grad_up = (grad_hidden * silu_value).astype(jnp.bfloat16)
    entry_grads = (
        contract_cols(grad_gate, gate_weight) + contract_cols(grad_up, up_weight)
    ).astype(jnp.bfloat16)
    back_rows = lax.all_to_all(
        entry_grads.reshape(groups, capacity, width),
        "expert",
        split_axis=0,
        concat_axis=0,
        tiled=True,
    )
    per_back = jnp.take(back_rows.reshape(groups * capacity, width), position, axis=0).reshape(
        tok_rows, top_count, width
    )
    token_grad = jnp.sum(per_back.astype(jnp.float32), axis=1).astype(jnp.bfloat16)
    grad_both = jnp.concatenate([grad_gate, grad_up], axis=1)
    share_rows = width // lax.axis_size("shard")
    shares = lax.psum_scatter(
        jnp.concatenate(
            [contract_rows(rows_x, grad_both), contract_rows(dout_rows, hidden)], axis=1
        ).astype(jnp.bfloat16),
        "shard",
        scatter_dimension=0,
        tiled=True,
    )
    shares = jnp.where(take_other, shifted(shares, "expert", halfway), shares).astype(jnp.float32)
    grad_in = jnp.transpose(
        shares[:, : 2 * hidden_width].reshape(share_rows, 2, hidden_width), (1, 0, 2)
    )[None]
    grad_down = jnp.transpose(shares[:, 2 * hidden_width :])[None]
    new_in, first_in, second_in = adam_update(kept_in, own_moments[0], own_moments[1], grad_in)
    new_down, first_down, second_down = adam_update(
        kept_down, own_moments[2], own_moments[3], grad_down
    )
    return (mixed, token_grad, new_in, new_down, first_in, second_in, first_down, second_down)


def solution(mesh):
    placed = (
        P(("expert", "shard"), None),
        P(("expert", "shard"), None),
        P(("expert", "shard"), None),
        P(),
        P("expert", None, "shard", None),
        P("expert", None, "shard"),
        P("expert", None, "shard", None),
        P("expert", None, "shard", None),
        P("expert", None, "shard"),
        P("expert", None, "shard"),
        P(("expert", "shard"), None),
    )
    return jax.shard_map(
        body,
        mesh=mesh,
        in_specs=placed,
        out_specs=(
            P(("expert", "shard"), None),
            P(("expert", "shard"), None),
            P("expert", None, "shard", None),
            P("expert", None, "shard"),
            P("expert", None, "shard", None),
            P("expert", None, "shard", None),
            P("expert", None, "shard"),
            P("expert", None, "shard"),
        ),
        check_vma=False,
    )
```

```python
import jax
import jax.numpy as jnp
from jax import lax
from jax.experimental import pallas as pl
from jax.experimental.pallas import tpu as pltpu
from jax.sharding import PartitionSpec as P
import functools

beta_first = 0.9
beta_second = 0.999
learn_rate = 0.01
adam_eps = 1e-08
bias_first = 0.9999734386011124
bias_second = 0.09520785288629038


def shifted(block, axis, distance):
    devices = range(lax.axis_size(axis))
    route = [((i - distance) % len(devices), i) for i in devices]
    return lax.ppermute(block, axis, route)


def exchange_kernel(count, spread, width, *refs):
    sources, targets = refs[:width], refs[width : 2 * width]
    send_sems, recv_sems, local_sems = refs[2 * width :]
    me = lax.axis_index("shard")
    row = lax.axis_index("expert")
    mesh_ids = pl.DeviceIdType.MESH
    barrier = pltpu.get_barrier_semaphore()
    for k in range(1, count):
        pl.semaphore_signal(
            barrier, inc=1, device_id=(row, lax.rem(me + k, count)), device_id_type=mesh_ids
        )
    pl.semaphore_wait(barrier, count - 1)
    copies = []
    for a in range(width):
        own = sources[a] if spread else sources[a].at[me]
        local = pltpu.make_async_copy(own, targets[a].at[me], local_sems.at[a])
        local.start()
        copies.append(local)
        for k in range(1, count):
            peer = lax.rem(me + k, count)
            remote = pltpu.make_async_remote_copy(
                src_ref=sources[a] if spread else sources[a].at[peer],
                dst_ref=targets[a].at[me],
                send_sem=send_sems.at[a, k - 1],
                recv_sem=recv_sems.at[a, k - 1],
                device_id=(row, peer),
                device_id_type=mesh_ids,
            )
            remote.start()
            copies.append(remote)
    for copy in copies:
        copy.wait()


def exchange(blocks, spread, ident):
    count = lax.axis_size("shard")
    width = len(blocks)
    shapes = tuple(
        jax.ShapeDtypeStruct((count,) + b.shape if spread else b.shape, b.dtype) for b in blocks
    )
    moved = sum(b.size * b.dtype.itemsize for b in blocks)
    return pl.pallas_call(
        functools.partial(exchange_kernel, count, spread, width),
        out_shape=shapes,
        in_specs=[pl.BlockSpec(memory_space=pl.ANY)] * width,
        out_specs=tuple(pl.BlockSpec(memory_space=pl.ANY) for _ in blocks),
        scratch_shapes=[
            pltpu.SemaphoreType.DMA((width, count - 1)),
            pltpu.SemaphoreType.DMA((width, count - 1)),
            pltpu.SemaphoreType.DMA((width,)),
        ],
        compiler_params=pltpu.CompilerParams(collective_id=ident, has_side_effects=True),
        cost_estimate=pl.CostEstimate(
            flops=0, transcendentals=0, bytes_accessed=2 * moved * (count if spread else 1)
        ),
    )(*blocks)


def silu_parts(gate_pre):
    sigmoid_value = jax.nn.sigmoid(gate_pre)
    silu_value = gate_pre * sigmoid_value
    slope = sigmoid_value * (1.0 + gate_pre * (1.0 - sigmoid_value))
    return (silu_value, slope)


def adam_update(weight, first, second, grad):
    first_new = beta_first * first + (1.0 - beta_first) * grad
    second_new = beta_second * second + (1.0 - beta_second) * grad * grad
    update = learn_rate * (first_new / bias_first) / (jnp.sqrt(second_new / bias_second) + adam_eps)
    return ((weight.astype(jnp.float32) - update).astype(jnp.bfloat16), first_new, second_new)


def route_table(expert_ids, dest_rows, groups, capacity):
    entry_count = expert_ids.shape[0] * expert_ids.shape[1]
    flat_ids = expert_ids.reshape(entry_count)
    onehot = (flat_ids[:, None] == jnp.arange(groups, dtype=jnp.int32)[None, :]).astype(jnp.int32)
    before = jnp.cumsum(onehot, axis=0) - onehot
    slot_index = jnp.sum(before * onehot, axis=1)
    position = dest_rows.reshape(entry_count) * capacity + slot_index
    entry_index = jnp.arange(entry_count, dtype=jnp.int32)
    filler = jnp.full((groups * capacity,), -1, jnp.int32).at[position].set(entry_index)
    return (position, filler)


def fill_rows(source_rows, filler, groups, capacity):
    picked = jnp.take(source_rows, jnp.maximum(filler, 0), axis=0)
    kept = jnp.where((filler >= 0)[:, None], picked, jnp.zeros_like(picked))
    return kept.reshape(groups, capacity, source_rows.shape[1])


def contract_rows(left, right):
    return lax.dot_general(
        left, right, (((0,), (0,)), ((), ())), preferred_element_type=jnp.float32
    )


def contract_cols(left, right):
    return lax.dot_general(
        left, right, (((1,), (1,)), ((), ())), preferred_element_type=jnp.float32
    )


def body(
    tokens, expert_ids, route_weights, partner, w_in, w_down, m_in, v_in, m_down, v_down, cotangent
):
    groups = lax.axis_size("expert")
    halfway = groups // 2
    tok_rows = tokens.shape[0]
    width = tokens.shape[1]
    top_count = expert_ids.shape[1]
    capacity = 3 * tok_rows * top_count // (2 * groups)
    row_index = lax.axis_index("expert")
    expert_range = jnp.arange(groups, dtype=jnp.int32)
    own_partner = jnp.sum(jnp.where(expert_range == row_index, partner, 0))
    take_other = own_partner != row_index
    moved_weights = shifted((w_in, w_down), "expert", halfway)
    w_in, w_down = (
        jnp.where(take_other, moved, owned) for moved, owned in zip(moved_weights, (w_in, w_down))
    )
    moved_states = tuple(
        shifted(state.astype(jnp.bfloat16), "expert", halfway).astype(state.dtype)
        for state in (m_in, v_in, m_down, v_down)
    )
    m_in, v_in, m_down, v_down = (
        jnp.where(take_other, moved, owned)
        for moved, owned in zip(moved_states, (m_in, v_in, m_down, v_down))
    )
    in_full, down_full = (
        lax.all_gather(w_in, "shard", axis=2, tiled=True),
        lax.all_gather(w_down, "shard", axis=2, tiled=True),
    )
    gate_weight = in_full[0, 0]
    up_weight = in_full[0, 1]
    down_weight = down_full[0]
    hidden_width = gate_weight.shape[1]
    position, filler = route_table(expert_ids, partner[expert_ids], groups, capacity)
    token_fill = jnp.where(filler >= 0, filler // top_count, -1)
    send_rows = fill_rows(tokens, token_fill, groups, capacity)
    arrived = lax.all_to_all(send_rows, "expert", split_axis=0, concat_axis=0, tiled=True)
    rows_x = arrived.reshape(groups * capacity, width)
    own_moments = (m_in, v_in, m_down, v_down)
    gate_pre = jnp.dot(rows_x, gate_weight, preferred_element_type=jnp.float32)
    up_pre = jnp.dot(rows_x, up_weight, preferred_element_type=jnp.float32)
    silu_value, slope = silu_parts(gate_pre)
    hidden = (silu_value * up_pre).astype(jnp.bfloat16)
    expert_out = jnp.dot(hidden, down_weight, preferred_element_type=jnp.float32).astype(
        jnp.bfloat16
    )
    returned = lax.all_to_all(
        expert_out.reshape(groups, capacity, width),
        "expert",
        split_axis=0,
        concat_axis=0,
        tiled=True,
    )
    per_entry = jnp.take(returned.reshape(groups * capacity, width), position, axis=0).reshape(
        tok_rows, top_count, width
    )
    mixed = jnp.sum(route_weights[:, :, None] * per_entry.astype(jnp.float32), axis=1).astype(
        jnp.bfloat16
    )
    scaled = (route_weights[:, :, None] * cotangent[:, None, :].astype(jnp.float32)).astype(
        jnp.bfloat16
    )
    send_grads = fill_rows(scaled.reshape(tok_rows * top_count, width), filler, groups, capacity)
    dout_rows = lax.all_to_all(
        send_grads, "expert", split_axis=0, concat_axis=0, tiled=True
    ).reshape(groups * capacity, width)
    grad_hidden = contract_cols(dout_rows, down_weight)
    grad_gate = (grad_hidden * up_pre * slope).astype(jnp.bfloat16)
    grad_up = (grad_hidden * silu_value).astype(jnp.bfloat16)
    entry_grads = (
        contract_cols(grad_gate, gate_weight) + contract_cols(grad_up, up_weight)
    ).astype(jnp.bfloat16)
    back_rows = lax.all_to_all(
        entry_grads.reshape(groups, capacity, width),
        "expert",
        split_axis=0,
        concat_axis=0,
        tiled=True,
    )
    per_back = jnp.take(back_rows.reshape(groups * capacity, width), position, axis=0).reshape(
        tok_rows, top_count, width
    )
    token_grad = jnp.sum(per_back.astype(jnp.float32), axis=1).astype(jnp.bfloat16)
    grad_both = jnp.concatenate([grad_gate, grad_up], axis=1)
    share_rows = width // lax.axis_size("shard")
    down_part, in_part = lax.optimization_barrier(
        (
            contract_rows(dout_rows, hidden).astype(jnp.bfloat16),
            contract_rows(rows_x, grad_both).astype(jnp.bfloat16),
        )
    )
    down_share = lax.psum_scatter(
        down_part, "shard", scatter_dimension=0, tiled=True
    ).astype(jnp.float32)
    shard_count = lax.axis_size("shard")
    (arrived_parts,) = exchange(
        (in_part.reshape(shard_count, share_rows, in_part.shape[1]),), False, 1
    )
    in_share = jnp.sum(arrived_parts.astype(jnp.float32), axis=0)
    grad_in = jnp.transpose(in_share.reshape(share_rows, 2, hidden_width), (1, 0, 2))[None]
    grad_down = jnp.transpose(down_share)[None]
    new_in, first_in, second_in = adam_update(w_in, own_moments[0], own_moments[1], grad_in)
    new_down, first_down, second_down = adam_update(
        w_down, own_moments[2], own_moments[3], grad_down
    )
    return (mixed, token_grad, new_in, new_down, first_in, second_in, first_down, second_down)


def solution(mesh):
    placed = (
        P(("expert", "shard"), None),
        P(("expert", "shard"), None),
        P(("expert", "shard"), None),
        P(),
        P("expert", None, "shard", None),
        P("expert", None, "shard"),
        P("expert", None, "shard", None),
        P("expert", None, "shard", None),
        P("expert", None, "shard"),
        P("expert", None, "shard"),
        P(("expert", "shard"), None),
    )
    return jax.shard_map(
        body,
        mesh=mesh,
        in_specs=placed,
        out_specs=(
            P(("expert", "shard"), None),
            P(("expert", "shard"), None),
            P("expert", None, "shard", None),
            P("expert", None, "shard"),
            P("expert", None, "shard", None),
            P("expert", None, "shard", None),
            P("expert", None, "shard"),
            P("expert", None, "shard"),
        ),
        check_vma=False,
    )
```

```python
import jax
import jax.numpy as jnp
from jax import lax
from jax.experimental import pallas as pl
from jax.experimental.pallas import tpu as pltpu
from jax.sharding import PartitionSpec as P
import functools

beta_first = 0.9
beta_second = 0.999
learn_rate = 0.01
adam_eps = 1e-08
bias_first = 0.9999734386011124
bias_second = 0.09520785288629038


def shifted(block, axis, distance):
    devices = range(lax.axis_size(axis))
    route = [((i - distance) % len(devices), i) for i in devices]
    return lax.ppermute(block, axis, route)


def exchange_kernel(count, spread, width, *refs):
    sources, targets = refs[:width], refs[width : 2 * width]
    send_sems, recv_sems, local_sems = refs[2 * width :]
    me = lax.axis_index("shard")
    row = lax.axis_index("expert")
    mesh_ids = pl.DeviceIdType.MESH
    barrier = pltpu.get_barrier_semaphore()
    for k in range(1, count):
        pl.semaphore_signal(
            barrier, inc=1, device_id=(row, lax.rem(me + k, count)), device_id_type=mesh_ids
        )
    pl.semaphore_wait(barrier, count - 1)
    copies = []
    for a in range(width):
        own = sources[a] if spread else sources[a].at[me]
        local = pltpu.make_async_copy(own, targets[a].at[me], local_sems.at[a])
        local.start()
        copies.append(local)
        for k in range(1, count):
            peer = lax.rem(me + k, count)
            remote = pltpu.make_async_remote_copy(
                src_ref=sources[a] if spread else sources[a].at[peer],
                dst_ref=targets[a].at[me],
                send_sem=send_sems.at[a, k - 1],
                recv_sem=recv_sems.at[a, k - 1],
                device_id=(row, peer),
                device_id_type=mesh_ids,
            )
            remote.start()
            copies.append(remote)
    for copy in copies:
        copy.wait()


def exchange(blocks, spread, ident):
    count = lax.axis_size("shard")
    width = len(blocks)
    shapes = tuple(
        jax.ShapeDtypeStruct((count,) + b.shape if spread else b.shape, b.dtype) for b in blocks
    )
    moved = sum(b.size * b.dtype.itemsize for b in blocks)
    return pl.pallas_call(
        functools.partial(exchange_kernel, count, spread, width),
        out_shape=shapes,
        in_specs=[pl.BlockSpec(memory_space=pl.ANY)] * width,
        out_specs=tuple(pl.BlockSpec(memory_space=pl.ANY) for _ in blocks),
        scratch_shapes=[
            pltpu.SemaphoreType.DMA((width, count - 1)),
            pltpu.SemaphoreType.DMA((width, count - 1)),
            pltpu.SemaphoreType.DMA((width,)),
        ],
        compiler_params=pltpu.CompilerParams(collective_id=ident, has_side_effects=True),
        cost_estimate=pl.CostEstimate(
            flops=0, transcendentals=0, bytes_accessed=2 * moved * (count if spread else 1)
        ),
    )(*blocks)


def silu_parts(gate_pre):
    sigmoid_value = jax.nn.sigmoid(gate_pre)
    silu_value = gate_pre * sigmoid_value
    slope = sigmoid_value * (1.0 + gate_pre * (1.0 - sigmoid_value))
    return (silu_value, slope)


def adam_update(weight, first, second, grad):
    first_new = beta_first * first + (1.0 - beta_first) * grad
    second_new = beta_second * second + (1.0 - beta_second) * grad * grad
    update = learn_rate * (first_new / bias_first) / (jnp.sqrt(second_new / bias_second) + adam_eps)
    return ((weight.astype(jnp.float32) - update).astype(jnp.bfloat16), first_new, second_new)


def route_table(expert_ids, dest_rows, groups, capacity):
    entry_count = expert_ids.shape[0] * expert_ids.shape[1]
    flat_ids = expert_ids.reshape(entry_count)
    onehot = (flat_ids[:, None] == jnp.arange(groups, dtype=jnp.int32)[None, :]).astype(jnp.int32)
    before = jnp.cumsum(onehot, axis=0) - onehot
    slot_index = jnp.sum(before * onehot, axis=1)
    position = dest_rows.reshape(entry_count) * capacity + slot_index
    entry_index = jnp.arange(entry_count, dtype=jnp.int32)
    filler = jnp.full((groups * capacity,), -1, jnp.int32).at[position].set(entry_index)
    return (position, filler)


def fill_rows(source_rows, filler, groups, capacity):
    picked = jnp.take(source_rows, jnp.maximum(filler, 0), axis=0)
    kept = jnp.where((filler >= 0)[:, None], picked, jnp.zeros_like(picked))
    return kept.reshape(groups, capacity, source_rows.shape[1])


def contract_rows(left, right):
    return lax.dot_general(
        left, right, (((0,), (0,)), ((), ())), preferred_element_type=jnp.float32
    )


def contract_cols(left, right):
    return lax.dot_general(
        left, right, (((1,), (1,)), ((), ())), preferred_element_type=jnp.float32
    )


def body(
    tokens, expert_ids, route_weights, partner, w_in, w_down, m_in, v_in, m_down, v_down, cotangent
):
    groups = lax.axis_size("expert")
    halfway = groups // 2
    tok_rows = tokens.shape[0]
    width = tokens.shape[1]
    top_count = expert_ids.shape[1]
    capacity = 3 * tok_rows * top_count // (2 * groups)
    row_index = lax.axis_index("expert")
    expert_range = jnp.arange(groups, dtype=jnp.int32)
    own_partner = jnp.sum(jnp.where(expert_range == row_index, partner, 0))
    take_other = own_partner != row_index
    moved_weights = shifted((w_in, w_down), "expert", halfway)
    w_in, w_down = (
        jnp.where(take_other, moved, owned) for moved, owned in zip(moved_weights, (w_in, w_down))
    )
    moved_states = tuple(
        shifted(state.astype(jnp.bfloat16), "expert", halfway).astype(state.dtype)
        for state in (m_in, v_in, m_down, v_down)
    )
    m_in, v_in, m_down, v_down = (
        jnp.where(take_other, moved, owned)
        for moved, owned in zip(moved_states, (m_in, v_in, m_down, v_down))
    )
    down_full = lax.all_gather(w_down, "shard", axis=2, tiled=True)
    gate_parts, up_parts = exchange((w_in[0, 0], w_in[0, 1]), True, 0)
    gate_weight = gate_parts.reshape(-1, gate_parts.shape[-1])
    up_weight = up_parts.reshape(-1, up_parts.shape[-1])
    down_weight = down_full[0]
    hidden_width = gate_weight.shape[1]
    position, filler = route_table(expert_ids, partner[expert_ids], groups, capacity)
    token_fill = jnp.where(filler >= 0, filler // top_count, -1)
    send_rows = fill_rows(tokens, token_fill, groups, capacity)
    arrived = lax.all_to_all(send_rows, "expert", split_axis=0, concat_axis=0, tiled=True)
    rows_x = arrived.reshape(groups * capacity, width)
    own_moments = (m_in, v_in, m_down, v_down)
    gate_pre = jnp.dot(rows_x, gate_weight, preferred_element_type=jnp.float32)
    up_pre = jnp.dot(rows_x, up_weight, preferred_element_type=jnp.float32)
    silu_value, slope = silu_parts(gate_pre)
    hidden = (silu_value * up_pre).astype(jnp.bfloat16)
    expert_out = jnp.dot(hidden, down_weight, preferred_element_type=jnp.float32).astype(
        jnp.bfloat16
    )
    returned = lax.all_to_all(
        expert_out.reshape(groups, capacity, width),
        "expert",
        split_axis=0,
        concat_axis=0,
        tiled=True,
    )
    per_entry = jnp.take(returned.reshape(groups * capacity, width), position, axis=0).reshape(
        tok_rows, top_count, width
    )
    mixed = jnp.sum(route_weights[:, :, None] * per_entry.astype(jnp.float32), axis=1).astype(
        jnp.bfloat16
    )
    scaled = (route_weights[:, :, None] * cotangent[:, None, :].astype(jnp.float32)).astype(
        jnp.bfloat16
    )
    send_grads = fill_rows(scaled.reshape(tok_rows * top_count, width), filler, groups, capacity)
    dout_rows = lax.all_to_all(
        send_grads, "expert", split_axis=0, concat_axis=0, tiled=True
    ).reshape(groups * capacity, width)
    grad_hidden = contract_cols(dout_rows, down_weight)
    grad_gate = (grad_hidden * up_pre * slope).astype(jnp.bfloat16)
    grad_up = (grad_hidden * silu_value).astype(jnp.bfloat16)
    entry_grads = (
        contract_cols(grad_gate, gate_weight) + contract_cols(grad_up, up_weight)
    ).astype(jnp.bfloat16)
    back_rows = lax.all_to_all(
        entry_grads.reshape(groups, capacity, width),
        "expert",
        split_axis=0,
        concat_axis=0,
        tiled=True,
    )
    per_back = jnp.take(back_rows.reshape(groups * capacity, width), position, axis=0).reshape(
        tok_rows, top_count, width
    )
    token_grad = jnp.sum(per_back.astype(jnp.float32), axis=1).astype(jnp.bfloat16)
    grad_both = jnp.concatenate([grad_gate, grad_up], axis=1)
    share_rows = width // lax.axis_size("shard")
    shares = lax.psum_scatter(
        jnp.concatenate(
            [contract_rows(rows_x, grad_both), contract_rows(dout_rows, hidden)], axis=1
        ).astype(jnp.bfloat16),
        "shard",
        scatter_dimension=0,
        tiled=True,
    ).astype(jnp.float32)
    grad_in = jnp.transpose(
        shares[:, : 2 * hidden_width].reshape(share_rows, 2, hidden_width), (1, 0, 2)
    )[None]
    grad_down = jnp.transpose(shares[:, 2 * hidden_width :])[None]
    new_in, first_in, second_in = adam_update(w_in, own_moments[0], own_moments[1], grad_in)
    new_down, first_down, second_down = adam_update(
        w_down, own_moments[2], own_moments[3], grad_down
    )
    return (mixed, token_grad, new_in, new_down, first_in, second_in, first_down, second_down)


def solution(mesh):
    placed = (
        P(("expert", "shard"), None),
        P(("expert", "shard"), None),
        P(("expert", "shard"), None),
        P(),
        P("expert", None, "shard", None),
        P("expert", None, "shard"),
        P("expert", None, "shard", None),
        P("expert", None, "shard", None),
        P("expert", None, "shard"),
        P("expert", None, "shard"),
        P(("expert", "shard"), None),
    )
    return jax.shard_map(
        body,
        mesh=mesh,
        in_specs=placed,
        out_specs=(
            P(("expert", "shard"), None),
            P(("expert", "shard"), None),
            P("expert", None, "shard", None),
            P("expert", None, "shard"),
            P("expert", None, "shard", None),
            P("expert", None, "shard", None),
            P("expert", None, "shard"),
            P("expert", None, "shard"),
        ),
        check_vma=False,
    )
```

```python
import jax
import jax.numpy as jnp
from jax import lax
from jax.experimental import pallas as pl
from jax.experimental.pallas import tpu as pltpu
from jax.sharding import PartitionSpec as P
import functools

beta_first = 0.9
beta_second = 0.999
learn_rate = 0.01
adam_eps = 1e-08
bias_first = 0.9999734386011124
bias_second = 0.09520785288629038


def shifted(block, axis, distance):
    devices = range(lax.axis_size(axis))
    route = [((i - distance) % len(devices), i) for i in devices]
    return lax.ppermute(block, axis, route)


def exchange_kernel(count, spread, width, *refs):
    sources, targets = refs[:width], refs[width : 2 * width]
    send_sems, recv_sems, local_sems = refs[2 * width :]
    me = lax.axis_index("shard")
    row = lax.axis_index("expert")
    mesh_ids = pl.DeviceIdType.MESH
    barrier = pltpu.get_barrier_semaphore()
    for k in range(1, count):
        pl.semaphore_signal(
            barrier, inc=1, device_id=(row, lax.rem(me + k, count)), device_id_type=mesh_ids
        )
    pl.semaphore_wait(barrier, count - 1)
    copies = []
    for a in range(width):
        own = sources[a] if spread else sources[a].at[me]
        local = pltpu.make_async_copy(own, targets[a].at[me], local_sems.at[a])
        local.start()
        copies.append(local)
        for k in range(1, count):
            peer = lax.rem(me + k, count)
            remote = pltpu.make_async_remote_copy(
                src_ref=sources[a] if spread else sources[a].at[peer],
                dst_ref=targets[a].at[me],
                send_sem=send_sems.at[a, k - 1],
                recv_sem=recv_sems.at[a, k - 1],
                device_id=(row, peer),
                device_id_type=mesh_ids,
            )
            remote.start()
            copies.append(remote)
    for copy in copies:
        copy.wait()


def exchange(blocks, spread, ident):
    count = lax.axis_size("shard")
    width = len(blocks)
    shapes = tuple(
        jax.ShapeDtypeStruct((count,) + b.shape if spread else b.shape, b.dtype) for b in blocks
    )
    moved = sum(b.size * b.dtype.itemsize for b in blocks)
    return pl.pallas_call(
        functools.partial(exchange_kernel, count, spread, width),
        out_shape=shapes,
        in_specs=[pl.BlockSpec(memory_space=pl.ANY)] * width,
        out_specs=tuple(pl.BlockSpec(memory_space=pl.ANY) for _ in blocks),
        scratch_shapes=[
            pltpu.SemaphoreType.DMA((width, count - 1)),
            pltpu.SemaphoreType.DMA((width, count - 1)),
            pltpu.SemaphoreType.DMA((width,)),
        ],
        compiler_params=pltpu.CompilerParams(collective_id=ident, has_side_effects=True),
        cost_estimate=pl.CostEstimate(
            flops=0, transcendentals=0, bytes_accessed=2 * moved * (count if spread else 1)
        ),
    )(*blocks)


def silu_parts(gate_pre):
    sigmoid_value = jax.nn.sigmoid(gate_pre)
    silu_value = gate_pre * sigmoid_value
    slope = sigmoid_value * (1.0 + gate_pre * (1.0 - sigmoid_value))
    return (silu_value, slope)


def adam_update(weight, first, second, grad):
    first_new = beta_first * first + (1.0 - beta_first) * grad
    second_new = beta_second * second + (1.0 - beta_second) * grad * grad
    update = learn_rate * (first_new / bias_first) / (jnp.sqrt(second_new / bias_second) + adam_eps)
    return ((weight.astype(jnp.float32) - update).astype(jnp.bfloat16), first_new, second_new)


def route_table(expert_ids, dest_rows, groups, capacity):
    entry_count = expert_ids.shape[0] * expert_ids.shape[1]
    flat_ids = expert_ids.reshape(entry_count)
    onehot = (flat_ids[:, None] == jnp.arange(groups, dtype=jnp.int32)[None, :]).astype(jnp.int32)
    before = jnp.cumsum(onehot, axis=0) - onehot
    slot_index = jnp.sum(before * onehot, axis=1)
    position = dest_rows.reshape(entry_count) * capacity + slot_index
    entry_index = jnp.arange(entry_count, dtype=jnp.int32)
    filler = jnp.full((groups * capacity,), -1, jnp.int32).at[position].set(entry_index)
    return (position, filler)


def fill_rows(source_rows, filler, groups, capacity):
    picked = jnp.take(source_rows, jnp.maximum(filler, 0), axis=0)
    kept = jnp.where((filler >= 0)[:, None], picked, jnp.zeros_like(picked))
    return kept.reshape(groups, capacity, source_rows.shape[1])


def contract_rows(left, right):
    return lax.dot_general(
        left, right, (((0,), (0,)), ((), ())), preferred_element_type=jnp.float32
    )


def contract_cols(left, right):
    return lax.dot_general(
        left, right, (((1,), (1,)), ((), ())), preferred_element_type=jnp.float32
    )


def body(
    tokens, expert_ids, route_weights, partner, w_in, w_down, m_in, v_in, m_down, v_down, cotangent
):
    groups = lax.axis_size("expert")
    halfway = groups // 2
    tok_rows = tokens.shape[0]
    width = tokens.shape[1]
    top_count = expert_ids.shape[1]
    capacity = 3 * tok_rows * top_count // (2 * groups)
    row_index = lax.axis_index("expert")
    expert_range = jnp.arange(groups, dtype=jnp.int32)
    own_partner = jnp.sum(jnp.where(expert_range == row_index, partner, 0))
    take_other = own_partner != row_index
    moved_weights = shifted((w_in, w_down), "expert", halfway)
    w_in, w_down = (
        jnp.where(take_other, moved, owned) for moved, owned in zip(moved_weights, (w_in, w_down))
    )
    moved_states = tuple(
        shifted(state.astype(jnp.bfloat16), "expert", halfway).astype(state.dtype)
        for state in (m_in, v_in, m_down, v_down)
    )
    m_in, v_in, m_down, v_down = (
        jnp.where(take_other, moved, owned)
        for moved, owned in zip(moved_states, (m_in, v_in, m_down, v_down))
    )
    down_full = lax.all_gather(w_down, "shard", axis=2, tiled=True)
    gate_parts, up_parts = exchange((w_in[0, 0], w_in[0, 1]), True, 0)
    gate_weight = gate_parts.reshape(-1, gate_parts.shape[-1])
    up_weight = up_parts.reshape(-1, up_parts.shape[-1])
    down_weight = down_full[0]
    hidden_width = gate_weight.shape[1]
    position, filler = route_table(expert_ids, partner[expert_ids], groups, capacity)
    token_fill = jnp.where(filler >= 0, filler // top_count, -1)
    send_rows = fill_rows(tokens, token_fill, groups, capacity)
    send_rows, w_in, w_down = lax.optimization_barrier((send_rows, w_in, w_down))
    arrived = lax.all_to_all(send_rows, "expert", split_axis=0, concat_axis=0, tiled=True)
    rows_x = arrived.reshape(groups * capacity, width)
    own_moments = (m_in, v_in, m_down, v_down)
    gate_pre = jnp.dot(rows_x, gate_weight, preferred_element_type=jnp.float32)
    up_pre = jnp.dot(rows_x, up_weight, preferred_element_type=jnp.float32)
    silu_value, slope = silu_parts(gate_pre)
    hidden = (silu_value * up_pre).astype(jnp.bfloat16)
    expert_out = jnp.dot(hidden, down_weight, preferred_element_type=jnp.float32).astype(
        jnp.bfloat16
    )
    returned = lax.all_to_all(
        expert_out.reshape(groups, capacity, width),
        "expert",
        split_axis=0,
        concat_axis=0,
        tiled=True,
    )
    per_entry = jnp.take(returned.reshape(groups * capacity, width), position, axis=0).reshape(
        tok_rows, top_count, width
    )
    mixed = jnp.sum(route_weights[:, :, None] * per_entry.astype(jnp.float32), axis=1).astype(
        jnp.bfloat16
    )
    scaled = (route_weights[:, :, None] * cotangent[:, None, :].astype(jnp.float32)).astype(
        jnp.bfloat16
    )
    send_grads = fill_rows(scaled.reshape(tok_rows * top_count, width), filler, groups, capacity)
    dout_rows = lax.all_to_all(
        send_grads, "expert", split_axis=0, concat_axis=0, tiled=True
    ).reshape(groups * capacity, width)
    grad_hidden = contract_cols(dout_rows, down_weight)
    grad_gate = (grad_hidden * up_pre * slope).astype(jnp.bfloat16)
    grad_up = (grad_hidden * silu_value).astype(jnp.bfloat16)
    entry_grads = (
        contract_cols(grad_gate, gate_weight) + contract_cols(grad_up, up_weight)
    ).astype(jnp.bfloat16)
    back_rows = lax.all_to_all(
        entry_grads.reshape(groups, capacity, width),
        "expert",
        split_axis=0,
        concat_axis=0,
        tiled=True,
    )
    per_back = jnp.take(back_rows.reshape(groups * capacity, width), position, axis=0).reshape(
        tok_rows, top_count, width
    )
    token_grad = jnp.sum(per_back.astype(jnp.float32), axis=1).astype(jnp.bfloat16)
    grad_both = jnp.concatenate([grad_gate, grad_up], axis=1)
    share_rows = width // lax.axis_size("shard")
    shares = lax.psum_scatter(
        jnp.concatenate(
            [contract_rows(rows_x, grad_both), contract_rows(dout_rows, hidden)], axis=1
        ).astype(jnp.bfloat16),
        "shard",
        scatter_dimension=0,
        tiled=True,
    ).astype(jnp.float32)
    grad_in = jnp.transpose(
        shares[:, : 2 * hidden_width].reshape(share_rows, 2, hidden_width), (1, 0, 2)
    )[None]
    grad_down = jnp.transpose(shares[:, 2 * hidden_width :])[None]
    new_in, first_in, second_in = adam_update(w_in, own_moments[0], own_moments[1], grad_in)
    new_down, first_down, second_down = adam_update(
        w_down, own_moments[2], own_moments[3], grad_down
    )
    return (mixed, token_grad, new_in, new_down, first_in, second_in, first_down, second_down)


def solution(mesh):
    placed = (
        P(("expert", "shard"), None),
        P(("expert", "shard"), None),
        P(("expert", "shard"), None),
        P(),
        P("expert", None, "shard", None),
        P("expert", None, "shard"),
        P("expert", None, "shard", None),
        P("expert", None, "shard", None),
        P("expert", None, "shard"),
        P("expert", None, "shard"),
        P(("expert", "shard"), None),
    )
    return jax.shard_map(
        body,
        mesh=mesh,
        in_specs=placed,
        out_specs=(
            P(("expert", "shard"), None),
            P(("expert", "shard"), None),
            P("expert", None, "shard", None),
            P("expert", None, "shard"),
            P("expert", None, "shard", None),
            P("expert", None, "shard", None),
            P("expert", None, "shard"),
            P("expert", None, "shard"),
        ),
        check_vma=False,
    )
```

```python
import jax
import jax.numpy as jnp
from jax import lax
from jax.sharding import PartitionSpec as P

beta_first = 0.9
beta_second = 0.999
learn_rate = 0.01
adam_eps = 1e-08
bias_first = 0.9999734386011124
bias_second = 0.09520785288629038


def shifted(block, axis, distance):
    devices = range(lax.axis_size(axis))
    route = [((i - distance) % len(devices), i) for i in devices]
    return lax.ppermute(block, axis, route)


def silu_parts(gate_pre):
    sigmoid_value = jax.nn.sigmoid(gate_pre)
    silu_value = gate_pre * sigmoid_value
    slope = sigmoid_value * (1.0 + gate_pre * (1.0 - sigmoid_value))
    return (silu_value, slope)


def adam_update(weight, first, second, grad):
    first_new = beta_first * first + (1.0 - beta_first) * grad
    second_new = beta_second * second + (1.0 - beta_second) * grad * grad
    update = learn_rate * (first_new / bias_first) / (jnp.sqrt(second_new / bias_second) + adam_eps)
    return ((weight.astype(jnp.float32) - update).astype(jnp.bfloat16), first_new, second_new)


def route_table(expert_ids, dest_rows, groups, capacity):
    entry_count = expert_ids.shape[0] * expert_ids.shape[1]
    flat_ids = expert_ids.reshape(entry_count)
    onehot = (flat_ids[:, None] == jnp.arange(groups, dtype=jnp.int32)[None, :]).astype(jnp.int32)
    before = jnp.cumsum(onehot, axis=0) - onehot
    slot_index = jnp.sum(before * onehot, axis=1)
    position = dest_rows.reshape(entry_count) * capacity + slot_index
    entry_index = jnp.arange(entry_count, dtype=jnp.int32)
    filler = jnp.full((groups * capacity,), -1, jnp.int32).at[position].set(entry_index)
    return (position, filler)


def fill_rows(source_rows, filler, groups, capacity):
    picked = jnp.take(source_rows, jnp.maximum(filler, 0), axis=0)
    kept = jnp.where((filler >= 0)[:, None], picked, jnp.zeros_like(picked))
    return kept.reshape(groups, capacity, source_rows.shape[1])


def contract_rows(left, right):
    return lax.dot_general(
        left, right, (((0,), (0,)), ((), ())), preferred_element_type=jnp.float32
    )


def contract_cols(left, right):
    return lax.dot_general(
        left, right, (((1,), (1,)), ((), ())), preferred_element_type=jnp.float32
    )


def body(
    tokens, expert_ids, route_weights, partner, w_in, w_down, m_in, v_in, m_down, v_down, cotangent
):
    groups = lax.axis_size("expert")
    halfway = groups // 2
    tok_rows = tokens.shape[0]
    width = tokens.shape[1]
    top_count = expert_ids.shape[1]
    capacity = 3 * tok_rows * top_count // (2 * groups)
    row_index = lax.axis_index("expert")
    expert_range = jnp.arange(groups, dtype=jnp.int32)
    own_partner = jnp.sum(jnp.where(expert_range == row_index, partner, 0))
    take_other = own_partner != row_index
    moved_weights = shifted((w_in, w_down), "expert", halfway)
    w_in, w_down = (
        jnp.where(take_other, moved, owned) for moved, owned in zip(moved_weights, (w_in, w_down))
    )
    moved_states = tuple(
        shifted(state.astype(jnp.bfloat16), "expert", halfway).astype(state.dtype)
        for state in (m_in, v_in, m_down, v_down)
    )
    m_in, v_in, m_down, v_down = (
        jnp.where(take_other, moved, owned)
        for moved, owned in zip(moved_states, (m_in, v_in, m_down, v_down))
    )
    in_full, down_full = (
        lax.all_gather(w_in, "shard", axis=2, tiled=True),
        lax.all_gather(w_down, "shard", axis=2, tiled=True),
    )
    gate_weight = in_full[0, 0]
    up_weight = in_full[0, 1]
    down_weight = down_full[0]
    hidden_width = gate_weight.shape[1]
    position, filler = route_table(expert_ids, partner[expert_ids], groups, capacity)
    token_fill = jnp.where(filler >= 0, filler // top_count, -1)
    send_rows = fill_rows(tokens, token_fill, groups, capacity)
    arrived = lax.all_to_all(send_rows, "expert", split_axis=0, concat_axis=0, tiled=True)
    rows_x = arrived.reshape(groups * capacity, width)
    own_moments = (m_in, v_in, m_down, v_down)
    gate_pre = jnp.dot(rows_x, gate_weight, preferred_element_type=jnp.float32)
    up_pre = jnp.dot(rows_x, up_weight, preferred_element_type=jnp.float32)
    silu_value, slope = silu_parts(gate_pre)
    hidden = (silu_value * up_pre).astype(jnp.bfloat16)
    expert_out = jnp.dot(hidden, down_weight, preferred_element_type=jnp.float32).astype(
        jnp.bfloat16
    )
    returned = lax.all_to_all(
        expert_out.reshape(groups, capacity, width),
        "expert",
        split_axis=0,
        concat_axis=0,
        tiled=True,
    )
    per_entry = jnp.take(returned.reshape(groups * capacity, width), position, axis=0).reshape(
        tok_rows, top_count, width
    )
    mixed = jnp.sum(route_weights[:, :, None] * per_entry.astype(jnp.float32), axis=1).astype(
        jnp.bfloat16
    )
    scaled = (route_weights[:, :, None] * cotangent[:, None, :].astype(jnp.float32)).astype(
        jnp.bfloat16
    )
    send_grads = fill_rows(scaled.reshape(tok_rows * top_count, width), filler, groups, capacity)
    dout_rows = lax.all_to_all(
        send_grads, "expert", split_axis=0, concat_axis=0, tiled=True
    ).reshape(groups * capacity, width)
    grad_hidden = contract_cols(dout_rows, down_weight)
    grad_gate = (grad_hidden * up_pre * slope).astype(jnp.bfloat16)
    grad_up = (grad_hidden * silu_value).astype(jnp.bfloat16)
    entry_grads = (
        contract_cols(grad_gate, gate_weight) + contract_cols(grad_up, up_weight)
    ).astype(jnp.bfloat16)
    back_rows = lax.all_to_all(
        entry_grads.reshape(groups, capacity, width),
        "expert",
        split_axis=0,
        concat_axis=0,
        tiled=True,
    )
    per_back = jnp.take(back_rows.reshape(groups * capacity, width), position, axis=0).reshape(
        tok_rows, top_count, width
    )
    token_grad = jnp.sum(per_back.astype(jnp.float32), axis=1).astype(jnp.bfloat16)
    grad_both = jnp.concatenate([grad_gate, grad_up], axis=1)
    share_rows = width // lax.axis_size("shard")
    partial = jnp.concatenate(
        [contract_rows(rows_x, grad_both), contract_rows(dout_rows, hidden)], axis=1
    ).astype(jnp.bfloat16)
    shard_count = lax.axis_size("shard")
    parts = lax.all_to_all(
        partial.reshape(shard_count, share_rows, partial.shape[1]),
        "shard",
        split_axis=0,
        concat_axis=0,
        tiled=True,
    )
    shares = jnp.sum(parts.astype(jnp.float32), axis=0)
    grad_in = jnp.transpose(
        shares[:, : 2 * hidden_width].reshape(share_rows, 2, hidden_width), (1, 0, 2)
    )[None]
    grad_down = jnp.transpose(shares[:, 2 * hidden_width :])[None]
    new_in, first_in, second_in = adam_update(w_in, own_moments[0], own_moments[1], grad_in)
    new_down, first_down, second_down = adam_update(
        w_down, own_moments[2], own_moments[3], grad_down
    )
    return (mixed, token_grad, new_in, new_down, first_in, second_in, first_down, second_down)


def solution(mesh):
    placed = (
        P(("expert", "shard"), None),
        P(("expert", "shard"), None),
        P(("expert", "shard"), None),
        P(),
        P("expert", None, "shard", None),
        P("expert", None, "shard"),
        P("expert", None, "shard", None),
        P("expert", None, "shard", None),
        P("expert", None, "shard"),
        P("expert", None, "shard"),
        P(("expert", "shard"), None),
    )
    return jax.shard_map(
        body,
        mesh=mesh,
        in_specs=placed,
        out_specs=(
            P(("expert", "shard"), None),
            P(("expert", "shard"), None),
            P("expert", None, "shard", None),
            P("expert", None, "shard"),
            P("expert", None, "shard", None),
            P("expert", None, "shard", None),
            P("expert", None, "shard"),
            P("expert", None, "shard"),
        ),
        check_vma=False,
    )
```

```python
import jax
import jax.numpy as jnp
from jax import lax
from jax.experimental import pallas as pl
from jax.experimental.pallas import tpu as pltpu
from jax.sharding import PartitionSpec as P
import functools

beta_first = 0.9
beta_second = 0.999
learn_rate = 0.01
adam_eps = 1e-08
bias_first = 0.9999734386011124
bias_second = 0.09520785288629038


def shifted(block, axis, distance):
    devices = range(lax.axis_size(axis))
    route = [((i - distance) % len(devices), i) for i in devices]
    return lax.ppermute(block, axis, route)


def exchange_kernel(count, spread, width, *refs):
    sources, targets = refs[:width], refs[width : 2 * width]
    send_sems, recv_sems, local_sems = refs[2 * width :]
    me = lax.axis_index("shard")
    row = lax.axis_index("expert")
    mesh_ids = pl.DeviceIdType.MESH
    barrier = pltpu.get_barrier_semaphore()
    for k in range(1, count):
        pl.semaphore_signal(
            barrier, inc=1, device_id=(row, lax.rem(me + k, count)), device_id_type=mesh_ids
        )
    pl.semaphore_wait(barrier, count - 1)
    copies = []
    for a in range(width):
        own = sources[a] if spread else sources[a].at[me]
        local = pltpu.make_async_copy(own, targets[a].at[me], local_sems.at[a])
        local.start()
        copies.append(local)
        for k in range(1, count):
            peer = lax.rem(me + k, count)
            remote = pltpu.make_async_remote_copy(
                src_ref=sources[a] if spread else sources[a].at[peer],
                dst_ref=targets[a].at[me],
                send_sem=send_sems.at[a, k - 1],
                recv_sem=recv_sems.at[a, k - 1],
                device_id=(row, peer),
                device_id_type=mesh_ids,
            )
            remote.start()
            copies.append(remote)
    for copy in copies:
        copy.wait()


def exchange(blocks, spread, ident):
    count = lax.axis_size("shard")
    width = len(blocks)
    shapes = tuple(
        jax.ShapeDtypeStruct((count,) + b.shape if spread else b.shape, b.dtype) for b in blocks
    )
    moved = sum(b.size * b.dtype.itemsize for b in blocks)
    return pl.pallas_call(
        functools.partial(exchange_kernel, count, spread, width),
        out_shape=shapes,
        in_specs=[pl.BlockSpec(memory_space=pl.ANY)] * width,
        out_specs=tuple(pl.BlockSpec(memory_space=pl.ANY) for _ in blocks),
        scratch_shapes=[
            pltpu.SemaphoreType.DMA((width, count - 1)),
            pltpu.SemaphoreType.DMA((width, count - 1)),
            pltpu.SemaphoreType.DMA((width,)),
        ],
        compiler_params=pltpu.CompilerParams(collective_id=ident, has_side_effects=True),
        cost_estimate=pl.CostEstimate(
            flops=0, transcendentals=0, bytes_accessed=2 * moved * (count if spread else 1)
        ),
    )(*blocks)


def silu_parts(gate_pre):
    sigmoid_value = jax.nn.sigmoid(gate_pre)
    silu_value = gate_pre * sigmoid_value
    slope = sigmoid_value * (1.0 + gate_pre * (1.0 - sigmoid_value))
    return (silu_value, slope)


def adam_update(weight, first, second, grad):
    first_new = beta_first * first + (1.0 - beta_first) * grad
    second_new = beta_second * second + (1.0 - beta_second) * grad * grad
    update = learn_rate * (first_new / bias_first) / (jnp.sqrt(second_new / bias_second) + adam_eps)
    return ((weight.astype(jnp.float32) - update).astype(jnp.bfloat16), first_new, second_new)


def route_table(expert_ids, dest_rows, groups, capacity):
    entry_count = expert_ids.shape[0] * expert_ids.shape[1]
    flat_ids = expert_ids.reshape(entry_count)
    onehot = (flat_ids[:, None] == jnp.arange(groups, dtype=jnp.int32)[None, :]).astype(jnp.int32)
    before = jnp.cumsum(onehot, axis=0) - onehot
    slot_index = jnp.sum(before * onehot, axis=1)
    position = dest_rows.reshape(entry_count) * capacity + slot_index
    entry_index = jnp.arange(entry_count, dtype=jnp.int32)
    filler = jnp.full((groups * capacity,), -1, jnp.int32).at[position].set(entry_index)
    return (position, filler)


def fill_rows(source_rows, filler, groups, capacity):
    picked = jnp.take(source_rows, jnp.maximum(filler, 0), axis=0)
    kept = jnp.where((filler >= 0)[:, None], picked, jnp.zeros_like(picked))
    return kept.reshape(groups, capacity, source_rows.shape[1])


def contract_rows(left, right):
    return lax.dot_general(
        left, right, (((0,), (0,)), ((), ())), preferred_element_type=jnp.float32
    )


def contract_cols(left, right):
    return lax.dot_general(
        left, right, (((1,), (1,)), ((), ())), preferred_element_type=jnp.float32
    )


def body(
    tokens, expert_ids, route_weights, partner, w_in, w_down, m_in, v_in, m_down, v_down, cotangent
):
    groups = lax.axis_size("expert")
    halfway = groups // 2
    tok_rows = tokens.shape[0]
    width = tokens.shape[1]
    top_count = expert_ids.shape[1]
    capacity = 3 * tok_rows * top_count // (2 * groups)
    row_index = lax.axis_index("expert")
    expert_range = jnp.arange(groups, dtype=jnp.int32)
    own_partner = jnp.sum(jnp.where(expert_range == row_index, partner, 0))
    take_other = own_partner != row_index
    moved_weights = shifted((w_in, w_down), "expert", halfway)
    w_in, w_down = (
        jnp.where(take_other, moved, owned) for moved, owned in zip(moved_weights, (w_in, w_down))
    )
    moved_states = tuple(
        shifted(state.astype(jnp.bfloat16), "expert", halfway).astype(state.dtype)
        for state in (m_in, v_in, m_down, v_down)
    )
    m_in, v_in, m_down, v_down = (
        jnp.where(take_other, moved, owned)
        for moved, owned in zip(moved_states, (m_in, v_in, m_down, v_down))
    )
    down_full = lax.all_gather(w_down, "shard", axis=2, tiled=True)
    gate_shard, up_shard, down_full = lax.optimization_barrier((w_in[0, 0], w_in[0, 1], down_full))
    gate_parts, up_parts = exchange((gate_shard, up_shard), True, 0)
    gate_weight = gate_parts.reshape(-1, gate_parts.shape[-1])
    up_weight = up_parts.reshape(-1, up_parts.shape[-1])
    down_weight = down_full[0]
    hidden_width = gate_weight.shape[1]
    position, filler = route_table(expert_ids, partner[expert_ids], groups, capacity)
    token_fill = jnp.where(filler >= 0, filler // top_count, -1)
    send_rows = fill_rows(tokens, token_fill, groups, capacity)
    send_rows, w_in, w_down = lax.optimization_barrier((send_rows, w_in, w_down))
    arrived = lax.all_to_all(send_rows, "expert", split_axis=0, concat_axis=0, tiled=True)
    rows_x = arrived.reshape(groups * capacity, width)
    own_moments = (m_in, v_in, m_down, v_down)
    gate_pre = jnp.dot(rows_x, gate_weight, preferred_element_type=jnp.float32)
    up_pre = jnp.dot(rows_x, up_weight, preferred_element_type=jnp.float32)
    silu_value, slope = silu_parts(gate_pre)
    hidden = (silu_value * up_pre).astype(jnp.bfloat16)
    expert_out = jnp.dot(hidden, down_weight, preferred_element_type=jnp.float32).astype(
        jnp.bfloat16
    )
    returned = lax.all_to_all(
        expert_out.reshape(groups, capacity, width),
        "expert",
        split_axis=0,
        concat_axis=0,
        tiled=True,
    )
    per_entry = jnp.take(returned.reshape(groups * capacity, width), position, axis=0).reshape(
        tok_rows, top_count, width
    )
    mixed = jnp.sum(route_weights[:, :, None] * per_entry.astype(jnp.float32), axis=1).astype(
        jnp.bfloat16
    )
    scaled = (route_weights[:, :, None] * cotangent[:, None, :].astype(jnp.float32)).astype(
        jnp.bfloat16
    )
    send_grads = fill_rows(scaled.reshape(tok_rows * top_count, width), filler, groups, capacity)
    dout_rows = lax.all_to_all(
        send_grads, "expert", split_axis=0, concat_axis=0, tiled=True
    ).reshape(groups * capacity, width)
    grad_hidden = contract_cols(dout_rows, down_weight)
    grad_gate = (grad_hidden * up_pre * slope).astype(jnp.bfloat16)
    grad_up = (grad_hidden * silu_value).astype(jnp.bfloat16)
    entry_grads = (
        contract_cols(grad_gate, gate_weight) + contract_cols(grad_up, up_weight)
    ).astype(jnp.bfloat16)
    back_rows = lax.all_to_all(
        entry_grads.reshape(groups, capacity, width),
        "expert",
        split_axis=0,
        concat_axis=0,
        tiled=True,
    )
    per_back = jnp.take(back_rows.reshape(groups * capacity, width), position, axis=0).reshape(
        tok_rows, top_count, width
    )
    token_grad = jnp.sum(per_back.astype(jnp.float32), axis=1).astype(jnp.bfloat16)
    grad_both = jnp.concatenate([grad_gate, grad_up], axis=1)
    share_rows = width // lax.axis_size("shard")
    shares = lax.psum_scatter(
        jnp.concatenate(
            [contract_rows(rows_x, grad_both), contract_rows(dout_rows, hidden)], axis=1
        ).astype(jnp.bfloat16),
        "shard",
        scatter_dimension=0,
        tiled=True,
    ).astype(jnp.float32)
    grad_in = jnp.transpose(
        shares[:, : 2 * hidden_width].reshape(share_rows, 2, hidden_width), (1, 0, 2)
    )[None]
    grad_down = jnp.transpose(shares[:, 2 * hidden_width :])[None]
    new_in, first_in, second_in = adam_update(w_in, own_moments[0], own_moments[1], grad_in)
    new_down, first_down, second_down = adam_update(
        w_down, own_moments[2], own_moments[3], grad_down
    )
    return (mixed, token_grad, new_in, new_down, first_in, second_in, first_down, second_down)


def solution(mesh):
    placed = (
        P(("expert", "shard"), None),
        P(("expert", "shard"), None),
        P(("expert", "shard"), None),
        P(),
        P("expert", None, "shard", None),
        P("expert", None, "shard"),
        P("expert", None, "shard", None),
        P("expert", None, "shard", None),
        P("expert", None, "shard"),
        P("expert", None, "shard"),
        P(("expert", "shard"), None),
    )
    return jax.shard_map(
        body,
        mesh=mesh,
        in_specs=placed,
        out_specs=(
            P(("expert", "shard"), None),
            P(("expert", "shard"), None),
            P("expert", None, "shard", None),
            P("expert", None, "shard"),
            P("expert", None, "shard", None),
            P("expert", None, "shard", None),
            P("expert", None, "shard"),
            P("expert", None, "shard"),
        ),
        check_vma=False,
    )
```

```python
import jax
import jax.numpy as jnp
from jax import lax
from jax.experimental import pallas as pl
from jax.experimental.pallas import tpu as pltpu
from jax.sharding import PartitionSpec as P
import functools

beta_first = 0.9
beta_second = 0.999
learn_rate = 0.01
adam_eps = 1e-08
bias_first = 0.9999734386011124
bias_second = 0.09520785288629038


def shifted(block, axis, distance):
    devices = range(lax.axis_size(axis))
    route = [((i - distance) % len(devices), i) for i in devices]
    return lax.ppermute(block, axis, route)


def exchange_kernel(count, spread, width, *refs):
    sources, targets = refs[:width], refs[width : 2 * width]
    send_sems, recv_sems, local_sems = refs[2 * width :]
    me = lax.axis_index("shard")
    row = lax.axis_index("expert")
    mesh_ids = pl.DeviceIdType.MESH
    barrier = pltpu.get_barrier_semaphore()
    for k in range(1, count):
        pl.semaphore_signal(
            barrier, inc=1, device_id=(row, lax.rem(me + k, count)), device_id_type=mesh_ids
        )
    pl.semaphore_wait(barrier, count - 1)
    copies = []
    for a in range(width):
        own = sources[a] if spread else sources[a].at[me]
        local = pltpu.make_async_copy(own, targets[a].at[me], local_sems.at[a])
        local.start()
        copies.append(local)
        for k in range(1, count):
            peer = lax.rem(me + k, count)
            remote = pltpu.make_async_remote_copy(
                src_ref=sources[a] if spread else sources[a].at[peer],
                dst_ref=targets[a].at[me],
                send_sem=send_sems.at[a, k - 1],
                recv_sem=recv_sems.at[a, k - 1],
                device_id=(row, peer),
                device_id_type=mesh_ids,
            )
            remote.start()
            copies.append(remote)
    for copy in copies:
        copy.wait()


def exchange(blocks, spread, ident):
    count = lax.axis_size("shard")
    width = len(blocks)
    shapes = tuple(
        jax.ShapeDtypeStruct((count,) + b.shape if spread else b.shape, b.dtype) for b in blocks
    )
    moved = sum(b.size * b.dtype.itemsize for b in blocks)
    return pl.pallas_call(
        functools.partial(exchange_kernel, count, spread, width),
        out_shape=shapes,
        in_specs=[pl.BlockSpec(memory_space=pl.ANY)] * width,
        out_specs=tuple(pl.BlockSpec(memory_space=pl.ANY) for _ in blocks),
        scratch_shapes=[
            pltpu.SemaphoreType.DMA((width, count - 1)),
            pltpu.SemaphoreType.DMA((width, count - 1)),
            pltpu.SemaphoreType.DMA((width,)),
        ],
        compiler_params=pltpu.CompilerParams(collective_id=ident, has_side_effects=True),
        cost_estimate=pl.CostEstimate(
            flops=0, transcendentals=0, bytes_accessed=2 * moved * (count if spread else 1)
        ),
    )(*blocks)


def silu_parts(gate_pre):
    sigmoid_value = jax.nn.sigmoid(gate_pre)
    silu_value = gate_pre * sigmoid_value
    slope = sigmoid_value * (1.0 + gate_pre * (1.0 - sigmoid_value))
    return (silu_value, slope)


def adam_update(weight, first, second, grad):
    first_new = beta_first * first + (1.0 - beta_first) * grad
    second_new = beta_second * second + (1.0 - beta_second) * grad * grad
    update = learn_rate * (first_new / bias_first) / (jnp.sqrt(second_new / bias_second) + adam_eps)
    return ((weight.astype(jnp.float32) - update).astype(jnp.bfloat16), first_new, second_new)


def route_table(expert_ids, dest_rows, groups, capacity):
    entry_count = expert_ids.shape[0] * expert_ids.shape[1]
    flat_ids = expert_ids.reshape(entry_count)
    onehot = (flat_ids[:, None] == jnp.arange(groups, dtype=jnp.int32)[None, :]).astype(jnp.int32)
    before = jnp.cumsum(onehot, axis=0) - onehot
    slot_index = jnp.sum(before * onehot, axis=1)
    position = dest_rows.reshape(entry_count) * capacity + slot_index
    entry_index = jnp.arange(entry_count, dtype=jnp.int32)
    filler = jnp.full((groups * capacity,), -1, jnp.int32).at[position].set(entry_index)
    return (position, filler)


def fill_rows(source_rows, filler, groups, capacity):
    picked = jnp.take(source_rows, jnp.maximum(filler, 0), axis=0)
    kept = jnp.where((filler >= 0)[:, None], picked, jnp.zeros_like(picked))
    return kept.reshape(groups, capacity, source_rows.shape[1])


def contract_rows(left, right):
    return lax.dot_general(
        left, right, (((0,), (0,)), ((), ())), preferred_element_type=jnp.float32
    )


def contract_cols(left, right):
    return lax.dot_general(
        left, right, (((1,), (1,)), ((), ())), preferred_element_type=jnp.float32
    )


def body(
    tokens, expert_ids, route_weights, partner, w_in, w_down, m_in, v_in, m_down, v_down, cotangent
):
    groups = lax.axis_size("expert")
    halfway = groups // 2
    tok_rows = tokens.shape[0]
    width = tokens.shape[1]
    top_count = expert_ids.shape[1]
    capacity = 3 * tok_rows * top_count // (2 * groups)
    row_index = lax.axis_index("expert")
    expert_range = jnp.arange(groups, dtype=jnp.int32)
    own_partner = jnp.sum(jnp.where(expert_range == row_index, partner, 0))
    take_other = own_partner != row_index
    moved_weights = shifted((w_in, w_down), "expert", halfway)
    w_in, w_down = (
        jnp.where(take_other, moved, owned) for moved, owned in zip(moved_weights, (w_in, w_down))
    )
    moved_states = tuple(
        shifted(state.astype(jnp.bfloat16), "expert", halfway).astype(state.dtype)
        for state in (m_in, v_in, m_down, v_down)
    )
    m_in, v_in, m_down, v_down = (
        jnp.where(take_other, moved, owned)
        for moved, owned in zip(moved_states, (m_in, v_in, m_down, v_down))
    )
    in_full = lax.all_gather(w_in, "shard", axis=2, tiled=True)
    gate_weight = in_full[0, 0]
    up_weight = in_full[0, 1]
    hidden_width = gate_weight.shape[1]
    position, filler = route_table(expert_ids, partner[expert_ids], groups, capacity)
    token_fill = jnp.where(filler >= 0, filler // top_count, -1)
    send_rows = fill_rows(tokens, token_fill, groups, capacity)
    arrived = lax.all_to_all(send_rows, "expert", split_axis=0, concat_axis=0, tiled=True)
    down_shard, arrived = lax.optimization_barrier((w_down[0], arrived))
    (down_parts,) = exchange((down_shard,), True, 0)
    down_weight = jnp.transpose(down_parts, (1, 0, 2)).reshape(down_parts.shape[1], -1)
    rows_x = arrived.reshape(groups * capacity, width)
    own_moments = (m_in, v_in, m_down, v_down)
    gate_pre = jnp.dot(rows_x, gate_weight, preferred_element_type=jnp.float32)
    up_pre = jnp.dot(rows_x, up_weight, preferred_element_type=jnp.float32)
    silu_value, slope = silu_parts(gate_pre)
    hidden = (silu_value * up_pre).astype(jnp.bfloat16)
    expert_out = jnp.dot(hidden, down_weight, preferred_element_type=jnp.float32).astype(
        jnp.bfloat16
    )
    returned = lax.all_to_all(
        expert_out.reshape(groups, capacity, width),
        "expert",
        split_axis=0,
        concat_axis=0,
        tiled=True,
    )
    per_entry = jnp.take(returned.reshape(groups * capacity, width), position, axis=0).reshape(
        tok_rows, top_count, width
    )
    mixed = jnp.sum(route_weights[:, :, None] * per_entry.astype(jnp.float32), axis=1).astype(
        jnp.bfloat16
    )
    scaled = (route_weights[:, :, None] * cotangent[:, None, :].astype(jnp.float32)).astype(
        jnp.bfloat16
    )
    send_grads = fill_rows(scaled.reshape(tok_rows * top_count, width), filler, groups, capacity)
    dout_rows = lax.all_to_all(
        send_grads, "expert", split_axis=0, concat_axis=0, tiled=True
    ).reshape(groups * capacity, width)
    grad_hidden = contract_cols(dout_rows, down_weight)
    grad_gate = (grad_hidden * up_pre * slope).astype(jnp.bfloat16)
    grad_up = (grad_hidden * silu_value).astype(jnp.bfloat16)
    entry_grads = (
        contract_cols(grad_gate, gate_weight) + contract_cols(grad_up, up_weight)
    ).astype(jnp.bfloat16)
    back_rows = lax.all_to_all(
        entry_grads.reshape(groups, capacity, width),
        "expert",
        split_axis=0,
        concat_axis=0,
        tiled=True,
    )
    per_back = jnp.take(back_rows.reshape(groups * capacity, width), position, axis=0).reshape(
        tok_rows, top_count, width
    )
    token_grad = jnp.sum(per_back.astype(jnp.float32), axis=1).astype(jnp.bfloat16)
    grad_both = jnp.concatenate([grad_gate, grad_up], axis=1)
    share_rows = width // lax.axis_size("shard")
    shares = lax.psum_scatter(
        jnp.concatenate(
            [contract_rows(rows_x, grad_both), contract_rows(dout_rows, hidden)], axis=1
        ).astype(jnp.bfloat16),
        "shard",
        scatter_dimension=0,
        tiled=True,
    ).astype(jnp.float32)
    grad_in = jnp.transpose(
        shares[:, : 2 * hidden_width].reshape(share_rows, 2, hidden_width), (1, 0, 2)
    )[None]
    grad_down = jnp.transpose(shares[:, 2 * hidden_width :])[None]
    new_in, first_in, second_in = adam_update(w_in, own_moments[0], own_moments[1], grad_in)
    new_down, first_down, second_down = adam_update(
        w_down, own_moments[2], own_moments[3], grad_down
    )
    return (mixed, token_grad, new_in, new_down, first_in, second_in, first_down, second_down)


def solution(mesh):
    placed = (
        P(("expert", "shard"), None),
        P(("expert", "shard"), None),
        P(("expert", "shard"), None),
        P(),
        P("expert", None, "shard", None),
        P("expert", None, "shard"),
        P("expert", None, "shard", None),
        P("expert", None, "shard", None),
        P("expert", None, "shard"),
        P("expert", None, "shard"),
        P(("expert", "shard"), None),
    )
    return jax.shard_map(
        body,
        mesh=mesh,
        in_specs=placed,
        out_specs=(
            P(("expert", "shard"), None),
            P(("expert", "shard"), None),
            P("expert", None, "shard", None),
            P("expert", None, "shard"),
            P("expert", None, "shard", None),
            P("expert", None, "shard", None),
            P("expert", None, "shard"),
            P("expert", None, "shard"),
        ),
        check_vma=False,
    )
```

```python
import jax
import jax.numpy as jnp
from jax import lax
from jax.sharding import PartitionSpec as P

beta_first = 0.9
beta_second = 0.999
learn_rate = 0.01
adam_eps = 1e-08
bias_first = 0.9999734386011124
bias_second = 0.09520785288629038


def shifted(block, axis, distance):
    devices = range(lax.axis_size(axis))
    route = [((i - distance) % len(devices), i) for i in devices]
    return lax.ppermute(block, axis, route)


def silu_parts(gate_pre):
    sigmoid_value = jax.nn.sigmoid(gate_pre)
    silu_value = gate_pre * sigmoid_value
    slope = sigmoid_value * (1.0 + gate_pre * (1.0 - sigmoid_value))
    return (silu_value, slope)


def adam_update(weight, first, second, grad):
    first_new = beta_first * first + (1.0 - beta_first) * grad
    second_new = beta_second * second + (1.0 - beta_second) * grad * grad
    update = learn_rate * (first_new / bias_first) / (jnp.sqrt(second_new / bias_second) + adam_eps)
    return ((weight.astype(jnp.float32) - update).astype(jnp.bfloat16), first_new, second_new)


def route_table(expert_ids, dest_rows, groups, capacity):
    entry_count = expert_ids.shape[0] * expert_ids.shape[1]
    flat_ids = expert_ids.reshape(entry_count)
    onehot = (flat_ids[:, None] == jnp.arange(groups, dtype=jnp.int32)[None, :]).astype(jnp.int32)
    before = jnp.cumsum(onehot, axis=0) - onehot
    slot_index = jnp.sum(before * onehot, axis=1)
    position = dest_rows.reshape(entry_count) * capacity + slot_index
    entry_index = jnp.arange(entry_count, dtype=jnp.int32)
    filler = jnp.full((groups * capacity,), -1, jnp.int32).at[position].set(entry_index)
    return (position, filler)


def fill_rows(source_rows, filler, groups, capacity):
    picked = jnp.take(source_rows, jnp.maximum(filler, 0), axis=0)
    kept = jnp.where((filler >= 0)[:, None], picked, jnp.zeros_like(picked))
    return kept.reshape(groups, capacity, source_rows.shape[1])


def contract_rows(left, right):
    return lax.dot_general(
        left, right, (((0,), (0,)), ((), ())), preferred_element_type=jnp.float32
    )


def contract_cols(left, right):
    return lax.dot_general(
        left, right, (((1,), (1,)), ((), ())), preferred_element_type=jnp.float32
    )


def body(
    tokens, expert_ids, route_weights, partner, w_in, w_down, m_in, v_in, m_down, v_down, cotangent
):
    groups = lax.axis_size("expert")
    halfway = groups // 2
    tok_rows = tokens.shape[0]
    width = tokens.shape[1]
    top_count = expert_ids.shape[1]
    capacity = 3 * tok_rows * top_count // (2 * groups)
    row_index = lax.axis_index("expert")
    expert_range = jnp.arange(groups, dtype=jnp.int32)
    own_partner = jnp.sum(jnp.where(expert_range == row_index, partner, 0))
    take_other = own_partner != row_index
    moved_weights = shifted((w_in, w_down), "expert", halfway)
    w_in, w_down = (
        jnp.where(take_other, moved, owned) for moved, owned in zip(moved_weights, (w_in, w_down))
    )
    moved_states = tuple(
        shifted(state.astype(jnp.bfloat16), "expert", halfway).astype(state.dtype)
        for state in (m_in, v_in, m_down, v_down)
    )
    m_in, v_in, m_down, v_down = (
        jnp.where(take_other, moved, owned)
        for moved, owned in zip(moved_states, (m_in, v_in, m_down, v_down))
    )
    in_full, down_full = (
        lax.all_gather(w_in, "shard", axis=2, tiled=True),
        lax.all_gather(w_down, "shard", axis=2, tiled=True),
    )
    gate_weight = in_full[0, 0]
    up_weight = in_full[0, 1]
    down_weight = down_full[0]
    hidden_width = gate_weight.shape[1]
    position, filler = route_table(expert_ids, partner[expert_ids], groups, capacity)
    token_fill = jnp.where(filler >= 0, filler // top_count, -1)
    send_rows = fill_rows(tokens, token_fill, groups, capacity)
    arrived = lax.all_to_all(send_rows, "expert", split_axis=0, concat_axis=0, tiled=True)
    rows_x = arrived.reshape(groups * capacity, width)
    own_moments = (m_in, v_in, m_down, v_down)
    gate_pre = jnp.dot(rows_x, gate_weight, preferred_element_type=jnp.float32)
    up_pre = jnp.dot(rows_x, up_weight, preferred_element_type=jnp.float32)
    silu_value, slope = silu_parts(gate_pre)
    hidden = (silu_value * up_pre).astype(jnp.bfloat16)
    expert_out = jnp.dot(hidden, down_weight, preferred_element_type=jnp.float32).astype(
        jnp.bfloat16
    )
    returned = lax.all_to_all(
        expert_out.reshape(groups, capacity, width),
        "expert",
        split_axis=0,
        concat_axis=0,
        tiled=True,
    )
    per_entry = jnp.take(returned.reshape(groups * capacity, width), position, axis=0).reshape(
        tok_rows, top_count, width
    )
    mixed = jnp.sum(route_weights[:, :, None] * per_entry.astype(jnp.float32), axis=1).astype(
        jnp.bfloat16
    )
    scaled = (route_weights[:, :, None] * cotangent[:, None, :].astype(jnp.float32)).astype(
        jnp.bfloat16
    )
    send_grads = fill_rows(scaled.reshape(tok_rows * top_count, width), filler, groups, capacity)
    dout_rows = lax.all_to_all(
        send_grads, "expert", split_axis=0, concat_axis=0, tiled=True
    ).reshape(groups * capacity, width)
    grad_hidden = contract_cols(dout_rows, down_weight)
    grad_gate = (grad_hidden * up_pre * slope).astype(jnp.bfloat16)
    grad_up = (grad_hidden * silu_value).astype(jnp.bfloat16)
    entry_grads = (
        contract_cols(grad_gate, gate_weight) + contract_cols(grad_up, up_weight)
    ).astype(jnp.bfloat16)
    back_rows = lax.all_to_all(
        entry_grads.reshape(groups, capacity, width),
        "expert",
        split_axis=0,
        concat_axis=0,
        tiled=True,
    )
    per_back = jnp.take(back_rows.reshape(groups * capacity, width), position, axis=0).reshape(
        tok_rows, top_count, width
    )
    token_grad = jnp.sum(per_back.astype(jnp.float32), axis=1).astype(jnp.bfloat16)
    grad_both = jnp.concatenate([grad_gate, grad_up], axis=1)
    share_rows = width // lax.axis_size("shard")
    in_share, down_share = lax.psum_scatter(
        (
            contract_rows(rows_x, grad_both).astype(jnp.bfloat16),
            contract_rows(dout_rows, hidden).astype(jnp.bfloat16),
        ),
        "shard",
        scatter_dimension=0,
        tiled=True,
    )
    grad_in = jnp.transpose(
        in_share.astype(jnp.float32).reshape(share_rows, 2, hidden_width), (1, 0, 2)
    )[None]
    grad_down = jnp.transpose(down_share.astype(jnp.float32))[None]
    new_in, first_in, second_in = adam_update(w_in, own_moments[0], own_moments[1], grad_in)
    new_down, first_down, second_down = adam_update(
        w_down, own_moments[2], own_moments[3], grad_down
    )
    return (mixed, token_grad, new_in, new_down, first_in, second_in, first_down, second_down)


def solution(mesh):
    placed = (
        P(("expert", "shard"), None),
        P(("expert", "shard"), None),
        P(("expert", "shard"), None),
        P(),
        P("expert", None, "shard", None),
        P("expert", None, "shard"),
        P("expert", None, "shard", None),
        P("expert", None, "shard", None),
        P("expert", None, "shard"),
        P("expert", None, "shard"),
        P(("expert", "shard"), None),
    )
    return jax.shard_map(
        body,
        mesh=mesh,
        in_specs=placed,
        out_specs=(
            P(("expert", "shard"), None),
            P(("expert", "shard"), None),
            P("expert", None, "shard", None),
            P("expert", None, "shard"),
            P("expert", None, "shard", None),
            P("expert", None, "shard", None),
            P("expert", None, "shard"),
            P("expert", None, "shard"),
        ),
        check_vma=False,
    )
```
